32 devices in a mesh: groups: 2 (over x), tensor: 16 (over z, y, core).
Axes of the slice: x: 2, y: 2, z: 4, core: 2. Of those that a mesh axis runs over, the one named last changes fastest.
Arguments:
- teacher_in: bfloat16 [1024, 5376], P(('groups', 'tensor')), parts along dimension 0, may hold values from -6 to 6
- gate_weight: bfloat16 [21504, 5376], P('tensor'), may hold values from -0.078125 to 0.078125
- up_weight: bfloat16 [21504, 5376], P('tensor'), may hold values from -0.078125 to 0.078125
- down_weight: bfloat16 [21504, 5376], P('tensor'), may hold values from -0.0546875 to 0.0546875
- post_gain: bfloat16 [5376], replicated, may hold values from 0.099609375 to 1.8984375
- student_in: bfloat16 [1024, 2560], P(('groups', 'tensor')), parts along dimension 0, may hold values from -6 to 6
- proj_weight: bfloat16 [5376, 2560], P('tensor'), may hold values from -0.125 to 0.125
Outputs:
- loss_value: float32 [2], P('groups'), parts along dimension 0
- proj_grad: float32 [10752, 2560], P(('groups', 'tensor')), parts along dimension 0
- student_grad: bfloat16 [1024, 2560], P(('groups', 'tensor')), parts along dimension 0
The draws below stay inside these ranges and needn't reach their ends.
There are 2 independent parts, one for each index of `groups`. The reference program is written for one: setup_inputs(seed, part) draws one part's arguments, and reference() takes and returns one part's arrays. A program takes and returns all parts, laid end to end along the dimension named above; an argument that names none is the same for every part. Nothing has to cross between parts.
All inputs are finite; a program needn't handle non-finite values.
Results may differ from the reference program's by a relative error of at most 0.0051.
Values may be sent and summed in bfloat16 or wider, within the bound.
A program may use at most 128 MiB of HBM per device.

```python
import jax
import jax.numpy as jnp
from jax import lax

D_T = 5376
FF = 21504
D_S = 2560
TOKENS = 512


def raised(drawn, key, source, target, parts, factor):
    owner, partner = [(jnp.arange(drawn.shape[dim]) // (drawn.shape[dim] // parts)).reshape([-1 if axis == dim else 1 for axis in range(drawn.ndim)]) for dim in (source, target)]
    chosen = jax.random.permutation(key, parts)[partner]
    strong = (owner == chosen) | (owner == (partner + parts // 2) % parts)
    return jnp.where(strong, factor * drawn, drawn)


def block_scale(stream_key, shape, cuts, low, high):
    def one(axis_at, blocks):
        heights = jax.random.uniform(jax.random.fold_in(jax.random.fold_in(stream_key, 6), axis_at), (blocks,), jnp.float32, low / len(cuts), high / len(cuts))
        return jnp.repeat(jnp.exp(heights), shape[axis_at] // blocks).reshape((-1,) + (1,) * (len(shape) - axis_at - 1))

    loudness = one(*cuts[0])
    for cut in cuts[1:]:
        loudness = loudness * one(*cut)
    return loudness


def noise(stream_key, shape, deviation, limit, pieces=(), kind=jnp.bfloat16):
    drawn = deviation * jax.random.normal(stream_key, shape, jnp.float32)
    if pieces:
        drawn = drawn * block_scale(stream_key, shape, pieces, -0.22, 0.18)
    return jnp.clip(drawn, -limit, limit).astype(kind)


def heavy_noise(stream_key, extent, width, reach, cuts, heavy, held_as=jnp.bfloat16):
    drawn = width * jax.random.normal(stream_key, extent, jnp.float32)
    if cuts:
        drawn = drawn * block_scale(stream_key, extent, cuts, -0.22, 0.18)
    return jnp.clip(raised(drawn, jax.random.fold_in(stream_key, 3), *heavy), -reach, reach).astype(held_as)


def setup_inputs(seed: int = 0, part: int = 0) -> dict:
    streams_of = jax.random.split(jax.random.key(seed), 8)
    part_splits = jax.random.split(jax.random.fold_in(streams_of[7], part), 8)
    teacher_in = noise(part_splits[0], (TOKENS, D_T), 1.0, 6.0, ((0, 16),))
    gate_weight = noise(streams_of[1], (FF, D_T), D_T ** -0.5, 0.078125, ((0, 16),))
    up_weight = noise(streams_of[2], (FF, D_T), D_T ** -0.5, 0.078125, ((0, 16),))
    down_weight = heavy_noise(streams_of[3], (FF, D_T), FF ** -0.5, 0.0546875, ((0, 16),), (0, 1, 16, 2.0))
    post_gain = jnp.clip(1.0 + 0.18 * jax.random.normal(streams_of[4], (D_T,), jnp.float32), 0.099609375, 1.8984375).astype(jnp.bfloat16)
    student_in = noise(part_splits[5], (TOKENS, D_S), 1.0, 6.0, ((0, 16),))
    proj_weight = noise(streams_of[6], (D_T, D_S), D_S ** -0.5, 0.125, ((0, 16),))
    return {"teacher_in": teacher_in, "gate_weight": gate_weight, "up_weight": up_weight, "down_weight": down_weight, "post_gain": post_gain, "student_in": student_in, "proj_weight": proj_weight}


def reference(teacher_in, gate_weight, up_weight, down_weight, post_gain, student_in, proj_weight):
    dims = (((1,), (1,)), ((), ()))
    gate_value = lax.dot_general(teacher_in, gate_weight, dims, preferred_element_type=jnp.float32)
    lift_value = lax.dot_general(teacher_in, up_weight, dims, preferred_element_type=jnp.float32)
    hidden = (jax.nn.gelu(gate_value, approximate=True) * lift_value).astype(jnp.bfloat16)
    ffn_out = jnp.dot(hidden, down_weight, preferred_element_type=jnp.float32)
    inv_norm = lax.rsqrt(lax.optimization_barrier(jnp.mean(ffn_out * ffn_out, axis=-1, keepdims=True)) + 1e-06)
    normed = ffn_out * inv_norm * post_gain.astype(jnp.float32)
    target = (teacher_in.astype(jnp.float32) + normed).astype(jnp.bfloat16)
    projected = lax.dot_general(student_in, proj_weight, dims, preferred_element_type=jnp.float32)
    difference = projected - target.astype(jnp.float32)
    loss_value = jnp.sum(difference * difference) / (TOKENS * D_T)
    cotangent = difference.astype(jnp.bfloat16)
    proj_grad = lax.dot_general(cotangent, student_in, (((0,), (0,)), ((), ())), preferred_element_type=jnp.float32)
    student_grad = jnp.dot(cotangent, proj_weight, preferred_element_type=jnp.float32).astype(jnp.bfloat16)
    return (jnp.reshape(loss_value, (1,)), proj_grad, student_grad)
```

```python
import functools

import jax
import jax.numpy as jnp
from jax import lax
from jax.experimental import pallas as pl
from jax.experimental.pallas import tpu as pltpu
from jax.sharding import PartitionSpec as P

epsilon = 1e-06
MESH = pl.DeviceIdType.MESH
f32 = jnp.float32
bf16 = jnp.bfloat16
by_last = (((1,), (1,)), ((), ()))

TEACHER = [(512, 'A'), (512, 'B'), (512, 'A'), (512, 'A'), (512, 'A'), (512, 'A'), (512, 'A'), (512, 'B'), (512, 'A'), (512, 'A'), (256, 'A')]
STUDENT = [(640, 'B'), (640, 'B'), (640, 'B'), (640, 'B')]
DOWN = [(32, 'B'), (32, 'A'), (32, 'A'), (32, 'A'), (32, 'A'), (32, 'B'), (32, 'A'), (32, 'A'), (32, 'A'), (32, 'A'), (16, 'A')]
GRAD = [(256, 'A'), (256, 'B'), (256, 'A'), (256, 'A'), (256, 'A'), (256, 'A'), (256, 'B'), (256, 'A'), (256, 'A'), (256, 'A')]
ORDER = [
    ("t", 0, 0), ("t", 1, 0), ("t", 2, 0), ("t", 3, 0), ("t", 4, 0), ("turn", 0, 0), ("turn", 1, 0),
    ("turn", 2, 0), ("turn", 3, 0), ("t", 0, 1), ("t", 0, 2), ("turn", 4, 0), ("turn", 5, 0), ("t", 1, 1),
    ("t", 2, 1), ("t", 2, 2), ("turn", 6, 0), ("t", 3, 1), ("t", 3, 2), ("turn", 7, 0), ("turn", 8, 0),
    ("t", 4, 1), ("t", 4, 2), ("turn", 9, 0), ("turn", 10, 0), ("t", 0, 3), ("t", 1, 2), ("turn", 11, 0),
    ("t", 1, 3), ("turn", 12, 0), ("turn", 13, 0), ("t", 5, 0), ("t", 2, 3), ("t", 3, 3), ("t", 4, 3),
    ("t", 0, 4), ("t", 1, 4), ("t", 6, 0), ("t", 7, 0), ("t", 5, 1), ("t", 5, 2), ("t", 2, 4), ("t", 0, 5),
    ("t", 3, 4), ("t", 4, 4), ("t", 0, 6), ("mul", 0, 0), ("mul", 0, 1), ("mul", 0, 2), ("t", 1, 5),
    ("t", 2, 5), ("t", 8, 0), ("mul", 0, 3), ("t", 3, 5), ("t", 6, 1), ("t", 6, 2), ("t", 5, 3), ("t", 4, 5),
    ("t", 7, 1), ("t", 1, 6), ("mul", 1, 0), ("t", 2, 6), ("t", 3, 6), ("t", 9, 0), ("mul", 1, 1),
    ("t", 4, 6), ("t", 6, 3), ("t", 8, 1), ("t", 8, 2), ("mul", 1, 2), ("t", 5, 4), ("mul", 1, 3),
    ("mul", 2, 0), ("t", 7, 2), ("t", 7, 3), ("mul", 2, 1), ("t", 10, 0), ("mul", 2, 2), ("t", 9, 1),
    ("t", 9, 2), ("mul", 2, 3), ("t", 5, 5), ("t", 6, 4), ("mul", 3, 0), ("t", 7, 4), ("t", 8, 3),
    ("mul", 3, 1), ("t", 5, 6), ("mul", 3, 2), ("t", 6, 5), ("mul", 3, 3), ("t", 10, 1), ("t", 10, 2),
    ("mul", 4, 0), ("t", 9, 3), ("t", 6, 6), ("mul", 4, 1), ("mul", 4, 2), ("mul", 4, 3), ("t", 7, 5),
    ("mul", 5, 0), ("t", 8, 4), ("t", 10, 3), ("mul", 5, 1), ("mul", 5, 2), ("t", 7, 6), ("t", 9, 4),
    ("t", 10, 4), ("s", 0, 0), ("s", 1, 0), ("mul", 5, 3), ("t", 8, 5), ("mul", 6, 0), ("s", 2, 0),
    ("mul", 6, 1), ("t", 9, 5), ("t", 10, 5), ("t", 8, 6), ("s", 3, 0), ("mul", 6, 2), ("mul", 6, 3),
    ("t", 9, 6), ("s", 0, 1), ("mul", 7, 0), ("t", 10, 6), ("s", 1, 1), ("mul", 7, 1), ("mul", 7, 2),
    ("s", 2, 1), ("mul", 7, 3), ("s", 3, 1), ("mul", 8, 0), ("mul", 8, 1), ("s", 0, 2), ("s", 0, 3),
    ("mul", 8, 2), ("mul", 8, 3), ("mul", 9, 0), ("s", 1, 2), ("s", 1, 3), ("mul", 9, 1), ("mul", 9, 2),
    ("mul", 9, 3), ("s", 2, 2), ("s", 2, 3), ("mul", 10, 0), ("mul", 10, 1), ("mul", 10, 2), ("s", 3, 2),
    ("s", 3, 3), ("mul", 10, 3), ("d", 0, 0), ("s", 0, 4), ("d", 1, 0), ("s", 1, 4), ("d", 2, 0), ("d", 0, 1),
    ("d", 3, 0), ("d", 1, 1), ("d", 2, 1), ("s", 2, 4), ("d", 4, 0), ("d", 3, 1), ("s", 3, 4), ("d", 5, 0),
    ("d", 4, 1), ("s", 0, 5), ("d", 6, 0), ("d", 1, 2), ("d", 7, 0), ("d", 0, 2), ("d", 5, 1), ("d", 6, 1),
    ("s", 0, 6), ("s", 1, 5), ("d", 8, 0), ("d", 7, 1), ("d", 2, 2), ("s", 2, 5), ("d", 9, 0), ("d", 1, 3),
    ("d", 8, 1), ("s", 1, 6), ("s", 3, 5), ("d", 10, 0), ("s", 2, 6), ("d", 0, 3), ("project", 0, 0),
    ("d", 9, 1), ("d", 3, 2), ("project", 1, 0), ("project", 2, 0), ("d", 10, 1), ("s", 3, 6),
    ("project", 3, 0), ("d", 1, 4), ("d", 0, 4), ("d", 5, 2), ("d", 1, 5), ("d", 4, 2), ("d", 2, 3),
    ("d", 5, 3), ("d", 3, 3), ("d", 2, 4), ("d", 4, 3), ("d", 3, 4), ("d", 4, 4), ("d", 6, 2), ("d", 6, 3),
    ("d", 6, 4), ("d", 5, 4), ("d", 7, 2), ("d", 7, 3), ("d", 2, 5), ("d", 3, 5), ("d", 8, 2), ("d", 8, 3),
    ("d", 4, 5), ("d", 7, 4), ("d", 8, 4), ("d", 9, 2), ("d", 9, 3), ("d", 6, 5), ("d", 10, 2), ("d", 10, 3),
    ("d", 0, 5), ("d", 5, 5), ("d", 7, 5), ("d", 8, 5), ("d", 9, 4), ("d", 10, 4), ("d", 9, 5), ("d", 10, 5),
    ("norm", 0, 0), ("g", 0, 0), ("g", 1, 0), ("g", 2, 0), ("g", 3, 0), ("g", 4, 0), ("g", 0, 1), ("g", 5, 0),
    ("g", 1, 1), ("g", 6, 0), ("g", 2, 1), ("g", 3, 1), ("g", 4, 1), ("g", 7, 0), ("g", 5, 1), ("g", 8, 0),
    ("g", 9, 0), ("g", 6, 1), ("pg", 0, 0), ("g", 0, 2), ("g", 7, 1), ("g", 8, 1), ("g", 9, 1), ("pg", 1, 0),
    ("g", 2, 2), ("pg", 2, 0), ("pg", 3, 0), ("g", 1, 2), ("g", 3, 2), ("g", 4, 2), ("g", 6, 2), ("g", 1, 3),
    ("g", 0, 3), ("g", 2, 3), ("g", 6, 3), ("g", 3, 3), ("g", 0, 4), ("g", 2, 4), ("g", 4, 3), ("g", 3, 4),
    ("g", 1, 4), ("g", 5, 2), ("g", 5, 3), ("g", 4, 4), ("g", 5, 4), ("g", 7, 2), ("g", 7, 3), ("g", 6, 4),
    ("g", 0, 5), ("g", 8, 2), ("g", 2, 5), ("g", 8, 3), ("g", 3, 5), ("g", 9, 2), ("g", 1, 5), ("g", 4, 5),
    ("g", 6, 5), ("g", 9, 3), ("g", 7, 4), ("g", 8, 4), ("g", 9, 4), ("g", 5, 5), ("g", 7, 5), ("g", 8, 5),
    ("g", 9, 5),
]
TURN = 384
VMEM_LIMIT = 58 * 2**20


class Place:
    def __init__(self):
        self.me = me = lax.axis_index("tensor")
        self.c = c = lax.rem(me, 2)
        self.y = y = lax.rem(me // 2, 2)
        self.z = z = me // 4
        self.low = z // 2
        odd = lax.rem(z, 2)
        self.mid = (z == 1) | (z == 2)
        self.end = (z == 0) | (z == 3)
        self.core = me + 1 - 2 * c
        self.across = me + 2 - 4 * y
        self.near_z = z + 1 - 2 * odd
        self.far_z = 3 - z
        self.other_mid = 2 - self.low
        self.other_end = 3 - 3 * self.low
        self.near = self.near_z * 4 + y * 2 + c
        self.far = self.far_z * 4 + y * 2 + c


class Wire:
    def __init__(self):
        self.owed = []

    def make(self, src, dst, send_sem, recv_sem, target):
        return pltpu.make_async_remote_copy(
            src_ref=src, dst_ref=dst, send_sem=send_sem, recv_sem=recv_sem,
            device_id={"tensor": target}, device_id_type=MESH,
        )

    def send(self, src, dst, send_sem, recv_sem, target, when=None):
        copy = self.make(src, dst, send_sem, recv_sem, target)
        if when is None:
            copy.start()
        else:
            pl.when(when)(copy.start)

    def arrived(self, like, recv_sem, target):
        self.make(like, like, recv_sem, recv_sem, target).wait_recv()

    def owe(self, like, send_sem, target, when=None):
        self.owed.append((when, self.make(like, like, send_sem, send_sem, target)))

    def flush(self):
        for when, copy in self.owed:
            if when is None:
                copy.wait_send()
            else:
                pl.when(when)(copy.wait_send)
        self.owed = []


class Gather:
    ops = 7

    def __init__(self, at, wire, order, own, buf, sems):
        self.at, self.wire, self.order, self.own, self.buf = at, wire, order, own, buf
        self.zn, self.zf, self.ys, self.yr, self.cs, self.cr, self.ls = (sems.at[i] for i in range(7))
        self.zr = [sems.at[7 + i] for i in range(3)]

    def row(self, z):
        if self.order == "A":
            return self.buf.at[z, self.at.y, self.at.c]
        return self.buf.at[z, :, self.at.c]

    def z_copy(self, z, land, target, src=None):
        row = self.row(z)
        sem = self.zn if target is self.at.near else self.zf
        return self.wire.make(row if src is None else src, row, sem, self.zr[land], target)

    def z_wait(self, z, land):
        self.wire.arrived(self.row(z), self.zr[land], self.at.near)

    def y_copy(self, z, src=None):
        at = self.at
        row = self.buf.at[z, at.y, at.c]
        return self.wire.make(row if src is None else src, row, self.ys, self.yr, at.across)

    def c_send(self, part):
        self.wire.send(part, part, self.cs, self.cr, self.at.core)

    def keep(self):
        at = self.at
        return pltpu.make_async_copy(self.own, self.buf.at[at.z, at.y, at.c], self.ls)

    def debts(self):
        at, buf, owe = self.at, self.buf, self.wire.owe
        owe(buf.at[:, at.y, at.c] if self.order == "A" else buf.at[at.z, at.y, at.c], self.ys, at.across)
        owe(buf.at[:, :, at.c], self.cs, at.core)
        owe(self.row(at.z), self.zn, at.near, when=at.end)
        owe(self.row(pl.ds(0, 3)), self.zn, at.near, when=at.mid)
        owe(self.row(pl.ds(0, 2)), self.zf, at.far, when=at.mid)

    def op(self, k):
        at = self.at
        if self.order == "A":
            self.op_a(k, at)
        else:
            self.op_b(k, at)
        if k == 6:
            self.debts()

    def pass_on(self, who, z, land, target=None, there=None):
        copies = []
        if target is not None:
            copies.append(self.z_copy(z, there, target))
        if self.order == "A":
            copies.append(self.y_copy(z))

        @pl.when(who)
        def _():
            self.z_wait(z, land)
            for copy in copies:
                copy.start()

    def op_a(self, k, at):
        buf = self.buf
        if k == 0:
            self.z_copy(at.z, 0, at.near, src=self.own).start()
            pl.when(at.mid)(self.z_copy(at.z, 1, at.far, src=self.own).start)
            self.y_copy(at.z, src=self.own).start()
            self.keep().start()
        elif k == 1:
            self.z_wait(at.near_z, 0)
            pl.when(at.mid)(self.z_copy(at.near_z, 2, at.far).start)
            self.y_copy(at.near_z).start()
        elif k == 2:
            self.pass_on(at.mid, at.other_mid, 1, at.near, 1)
        elif k == 3:
            self.pass_on(at.mid, at.other_end, 2, at.near, 2)
            self.pass_on(at.end, at.other_mid, 1)
        elif k == 4:
            self.pass_on(at.end, at.other_end, 2)
            self.keep().wait()
            self.c_send(buf.at[:, at.y, at.c])
        elif k == 5:
            self.wire.arrived(buf.at[:, 1 - at.y, at.c], self.yr, at.across)
            self.c_send(buf.at[:, 1 - at.y, at.c])
        else:
            self.wire.arrived(buf.at[:, :, 1 - at.c], self.cr, at.core)

    def op_b(self, k, at):
        buf = self.buf
        if k == 0:
            self.y_copy(at.z, src=self.own).start()
            self.keep().start()
        elif k == 1:
            self.keep().wait()
            self.wire.arrived(buf.at[at.z, 1 - at.y, at.c], self.yr, at.across)
            self.z_copy(at.z, 0, at.near).start()
            pl.when(at.mid)(self.z_copy(at.z, 1, at.far).start)
        elif k == 2:
            self.pass_on(at.mid, at.near_z, 0, at.far, 2)
        elif k == 3:
            self.pass_on(at.mid, at.other_mid, 1, at.near, 1)
        elif k == 4:
            self.pass_on(at.mid, at.other_end, 2, at.near, 2)
        elif k == 5:

            @pl.when(at.end)
            def _():
                self.z_wait(at.near_z, 0)
                self.z_wait(at.other_mid, 1)
                self.z_wait(at.other_end, 2)

            self.c_send(buf.at[:, :, at.c])
        else:
            self.wire.arrived(buf.at[:, :, 1 - at.c], self.cr, at.core)


class Reduce:
    ops = 6

    def __init__(self, at, wire, order, part, fill, finish, bufs, sems):
        self.at, self.wire, self.order = at, wire, order
        self.part, self.fill, self.finish = part, fill, finish
        self.r1, self.s1, self.yb, self.r2, self.go, self.rn, self.rf = bufs
        self.cs, self.ys, self.yr, self.ns, self.nr, self.fs, self.fr = (sems.at[i] for i in range(7))
        self.cr = [sems.at[7 + i] for i in range(2)]

    def debts(self):
        at, owe = self.at, self.wire.owe
        owe(self.r1, self.cs, at.core)
        owe(self.s1 if self.order == "A" else self.yb, self.ys, at.across)
        owe(self.go, self.ns, at.near, when=at.end)
        owe(self.go.at[pl.ds(2, 1)], self.ns, at.near, when=at.mid)
        owe(self.go.at[pl.ds(0, 2)], self.fs, at.far, when=at.mid)

    def op(self, k):
        at = self.at
        if k == 0:
            self.begin(at)
        elif self.order == "A":
            self.op_a(k, at)
        else:
            self.op_b(k, at)
        if k == 5:
            self.debts()

    def begin(self, at):
        self.fill()
        for i, y in enumerate((1 - at.y, at.y)):
            self.wire.send(self.part(y, 1 - at.c), self.r1.at[y], self.cs, self.cr[i], at.core)

    def c_wait(self, at, i):
        y = (1 - at.y, at.y)[i]
        self.wire.arrived(self.r1.at[y], self.cr[i], at.core)

    def two(self, y, zs):
        at = self.at
        return self.part(y, at.c)[zs].astype(f32) + self.r1[y, zs].astype(f32)

    def total(self, zs):
        at = self.at
        if self.order == "A":
            return self.two(at.y, zs) + self.r2[zs].astype(f32)
        return jnp.stack([self.two(y, zs) for y in range(2)], axis=1)

    def z_ops(self, k, at):
        go, rn, rf = self.go, self.rn, self.rf
        if k == 0:
            inward = self.wire.make(go, rn, self.ns, self.nr, at.near)

            @pl.when(at.end)
            def _():
                go[...] = self.total(pl.ds(1 - at.low, 3)).astype(bf16)
                inward.start()

        elif k == 1:
            onward = self.wire.make(go.at[pl.ds(0, 2)], rf, self.fs, self.fr, at.far)

            @pl.when(at.mid)
            def _():
                self.wire.arrived(rn, self.nr, at.near)
                there = self.total(pl.ds(2 - 2 * at.low, 2))
                go[0:2] = (there + rn[pl.ds(1 - at.low, 2)].astype(f32)).astype(bf16)
                onward.start()

        elif k == 2:
            back = self.wire.make(go.at[pl.ds(2, 1)], rn.at[pl.ds(0, 1)], self.ns, self.nr, at.near)

            @pl.when(at.mid)
            def _():
                self.wire.arrived(rf, self.fr, at.far)
                there = self.total(pl.ds(at.near_z, 1))
                go[2:3] = (there + rf[pl.ds(at.low, 1)].astype(f32)).astype(bf16)
                back.start()

    def own(self, at, done):
        rn, rf = self.rn, self.rf

        @pl.when(at.end)
        def _():
            self.wire.arrived(rn.at[pl.ds(0, 1)], self.nr, at.near)
            done((self.total(pl.ds(at.z, 1)) + rn[0:1].astype(f32))[0])

        @pl.when(at.mid)
        def _():
            done(
                (
                    self.total(pl.ds(at.z, 1))
                    + rn[pl.ds(2 * at.low, 1)].astype(f32)
                    + rf[pl.ds(1 - at.low, 1)].astype(f32)
                )[0]
            )

    def op_a(self, k, at):
        every = pl.ds(0, 4)
        if k == 1:
            self.c_wait(at, 0)
            self.s1[...] = self.two(1 - at.y, every).astype(bf16)
            self.wire.send(self.s1, self.r2, self.ys, self.yr, at.across)
        elif k == 2:
            self.c_wait(at, 1)
            self.wire.arrived(self.r2, self.yr, at.across)
            self.z_ops(0, at)
        elif k == 3:
            self.z_ops(1, at)
        elif k == 4:
            self.z_ops(2, at)
        else:
            self.own(at, self.finish)

    def op_b(self, k, at):
        if k == 1:
            self.c_wait(at, 0)
            self.c_wait(at, 1)
            self.z_ops(0, at)
        elif k == 2:
            self.z_ops(1, at)
        elif k == 3:
            self.z_ops(2, at)
        elif k == 4:

            def store(v):
                self.s1[...] = v

            self.own(at, store)
            self.yb[...] = self.s1[1 - at.y].astype(bf16)
            self.wire.send(self.yb, self.r2, self.ys, self.yr, at.across)
        else:
            self.wire.arrived(self.r2, self.yr, at.across)
            self.finish(self.s1[at.y] + self.r2[...].astype(f32))


def reduce_scratch(order, r, n):
    V = pltpu.VMEM
    D = pltpu.SemaphoreType.DMA
    two = () if order == "A" else (2,)
    bufs = [
        V((2, 4, r, n), bf16),
        V((4, r, n), bf16) if order == "A" else V((2, r, n), f32),
        V((16, 128) if order == "A" else (r, n), bf16),
        V((4, r, n), bf16) if order == "A" else V((r, n), bf16),
        V((3,) + two + (r, n), bf16), V((3,) + two + (r, n), bf16), V((2,) + two + (r, n), bf16),
    ]
    return bufs, D((9,))


def gather_scratch(n):
    D = pltpu.SemaphoreType.DMA
    return [pltpu.VMEM((4, 2, 2, 32, n), bf16)], D((10,))


def cut(pieces, whole):
    starts, at = [], 0
    for size, order in pieces:
        starts.append((at, size, order))
        at += size
    return starts if at == whole else None


def plan(K, S, F):
    return cut(TEACHER, K), cut(STUDENT, S), cut(DOWN, F), cut(GRAD, S)


def body(dims, shapes, *refs):
    x, st, gate, up, down, gain, proj, pg, sg, loss = refs[:10]
    take = iter(jax.tree.unflatten(shapes, refs[10:]))
    K, N, S, F, pad, fpad = dims
    teacher, student, downs, grads = plan(K, S, F)
    xa, xsems, xs, ssems, rbuf, rsem, qbuf, parts, wt = (next(take) for _ in range(9))
    (acc, hidden, wbuf, dbuf, ffn, base, gcol, projected, pbuf, gbuf, cot_t, cot,
     nb, nr, lb, lr, wsem, dsem, psem, gsem, ns_, nr_, ls_, lr_) = take
    at, wire = Place(), Wire()
    B = x.shape[0]
    T = 16
    R = T * B
    half = N // 2
    turns = K // TURN
    me = at.me

    def fetch(j):
        first, n, _ = teacher[j]
        return [
            pltpu.make_async_copy(
                w.at[:, pl.ds(first, n)], wbuf.at[i, j % 2, :, pl.ds(0, n)], wsem.at[i, j % 2]
            )
            for i, w in enumerate((gate, up))
        ]

    def fetch_down(i):
        return pltpu.make_async_copy(
            down.at[:, pl.ds(i * TURN, TURN)], dbuf.at[i % 2, pl.ds(0, N)], dsem.at[i % 2]
        )

    projector = pltpu.make_async_copy(proj, pbuf.at[pl.ds(0, F)], psem)
    gains = pltpu.make_async_copy(gain, gbuf, gsem)

    for j in range(2):
        for copy in fetch(j):
            copy.start()
        fetch_down(j).start()
    projector.start()
    gains.start()
    others = [lax.rem(me + k, T) for k in range(1, T)]
    barrier = pltpu.get_barrier_semaphore()
    for target in others:
        pl.semaphore_signal(barrier, inc=1, device_id={"tensor": target}, device_id_type=MESH)
    pl.semaphore_wait(barrier, T - 1)

    gathers = [
        Gather(at, Wire(), order, x.at[:, pl.ds(first, n)], xa[j], xsems[j])
        for j, (first, n, order) in enumerate(teacher)
    ] + [
        Gather(at, wire, order, st.at[:, pl.ds(first, n)], xs[j], ssems[j])
        for j, (first, n, order) in enumerate(student)
    ]

    def clear():
        dbuf[:, N:pad] = jnp.zeros((2, pad - N, TURN), bf16)
        hidden[N:pad] = jnp.zeros((pad - N, R), bf16)
        pbuf[F:fpad] = jnp.zeros((fpad - F, S), bf16)
        cot_t[F:fpad] = jnp.zeros((fpad - F, R), bf16)
        base[...] = jnp.zeros_like(base)
        gcol[...] = jnp.zeros_like(gcol)

    def held(which, part):
        q = which * 4 + part
        return pg.at[:, pl.ds(q * R, R)] if q < 5 else acc.at[q - 5]

    def multiply(j, i):
        first, n, _ = teacher[j]
        which, side = i % 2, i // 2
        if i == 0:
            for copy in fetch(j):
                copy.wait()

        @pl.loop(0, 1)
        def _(_):
            d = lax.dot_general(
                wbuf[which, j % 2, side * half : (side + 1) * half, 0:n], xa[j][...].reshape(R, n),
                by_last, preferred_element_type=f32,
            )
            for q in range(2):
                part = d[q * F : (q + 1) * F]
                place = held(which, side * 2 + q)
                if j > 0:
                    part += place[...]
                if j < len(teacher) - 1 or which == 0:
                    place[...] = part
                else:
                    rows = slice(side * half + q * F, side * half + (q + 1) * F)
                    value = held(0, side * 2 + q)[...]
                    hidden[rows] = (jax.nn.gelu(value, approximate=True) * part).astype(bf16)

        if i == 3:
            own_part(j)
            if j + 2 < len(teacher):
                for copy in fetch(j + 2):
                    copy.start()

    def one(rows, cols, off):
        i = lax.broadcasted_iota(jnp.int32, (rows, cols), 0)
        k = lax.broadcasted_iota(jnp.int32, (rows, cols), 1)
        return jnp.where(i == k + off, 1.0, 0.0).astype(bf16)

    def turn(i):
        fetch_down(i).wait()
        got = dbuf[i % 2].T
        row = 0
        while row < TURN:
            d, r = divmod(i * TURN + row, F)
            j = max(q for q, (first, _, _) in enumerate(downs) if first <= r)
            first, size, _ = downs[j]
            run = min(TURN - row, first + size - r)
            begin = d * size + r - first
            wt[j][begin : begin + run] = got[row : row + run]
            row += run
        if i + 2 < turns:
            fetch_down(i + 2).start()

    def own_part(j):
        first, n, _ = teacher[j]

        @pl.when((first < F * me + F) & (first + n > F * me))
        def _():
            sel = one(F, n, first - F * me)
            base[...] += lax.dot_general(
                sel, xa[j][...].reshape(R, n), by_last, preferred_element_type=f32
            )
            wide = jnp.broadcast_to(gbuf[first : first + n][None], (128, n))
            gcol[...] += lax.dot_general(sel, wide, by_last, preferred_element_type=f32)

    def project(j):
        first, n, _ = student[j]
        got = lax.dot_general(
            pbuf[0:F, first : first + n], xs[j][...].reshape(R, n), by_last,
            preferred_element_type=f32,
        )
        projected[...] = got if j == 0 else projected[...] + got

    def down_item(j):
        first, r, order = downs[j]

        held_by = parts[j] if j in parts else xa[j]

        def fill():
            if j not in parts:
                gathers[j].wire.flush()

            @pl.loop(0, 1)
            def _(_):
                got = jnp.dot(wt[j][...], hidden[...], preferred_element_type=f32)
                held_by[...] = got.astype(bf16).reshape(4, 2, 2, r, R)

        def finish(v):
            ffn[first : first + r] = v

        return Reduce(at, wire, order, lambda y, c: held_by.at[:, y, c], fill, finish, rbuf[j], rsem[j])

    def grad_item(j):
        first, n, order = grads[j]

        def fill():
            @pl.loop(0, 1)
            def _(_):
                got = jnp.dot(cot[...], pbuf[:, first : first + n], preferred_element_type=f32)
                xa[j][:, :, :, :, 0:n] = got.astype(bf16).reshape(4, 2, 2, B, n)

        def finish(v):
            sg[:, first : first + n] = v.astype(bf16)

        return Reduce(
            at, wire, order, lambda y, c: xa[j].at[:, y, c, :, pl.ds(0, n)], fill, finish,
            qbuf[j], rsem[j],
        )

    down_items = [down_item(j) for j in range(len(downs))]
    grad_items = [grad_item(j) for j in range(len(grads))]

    def everyone(src, dst, ss, rs):
        for v in others:
            wire.send(src, dst.at[me], ss, rs, v)
        dst[me] = src[...]
        wire.owe(dst.at[pl.ds(0, T - 1)], ss, others[0])

        def collect():
            wire.arrived(dst.at[pl.ds(0, T - 1)], rs, others[0])
            return jnp.sum(dst[...], axis=0)

        return collect

    def norm():
        whole = ffn[...]
        nb[...] = jnp.sum(whole * whole, axis=0, keepdims=True)
        collect = everyone(nb, nr, ns_, nr_)
        inv_norm = lax.rsqrt(collect() / K + epsilon)
        target = (base[...] + ffn[...] * inv_norm * gcol[:, 0:1]).astype(bf16)
        difference = projected[...] - target.astype(f32)
        lb[...] = jnp.sum(difference * difference, axis=0, keepdims=True)
        cot_t[0:F] = difference.astype(bf16)
        cot[...] = lax.dot_general(
            one(R, R, 0), cot_t[...], by_last, preferred_element_type=f32
        ).astype(bf16)
        for gather in gathers:
            gather.wire.flush()
        wire.flush()
        return everyone(lb, lr, ls_, lr_)

    def proj_grad(j):
        first, n, _ = student[j]
        pg[:, first : first + n] = jnp.dot(
            cot_t[0:F], xs[j][...].reshape(R, n), preferred_element_type=f32
        )

    calls = {
        "t": lambda j, k: gathers[j].op(k),
        "s": lambda j, k: gathers[len(teacher) + j].op(k),
        "d": lambda j, k: down_items[j].op(k),
        "g": lambda j, k: grad_items[j].op(k),
        "mul": multiply,
        "turn": lambda j, k: turn(j),
        "project": lambda j, k: project(j),
        "pg": lambda j, k: proj_grad(j),
    }
    started = False
    for what, j, k in ORDER:
        if what not in ("t", "s") and not started:
            started = True
            clear()
            projector.wait()
            gains.wait()
        if what == "norm":
            errors = norm()
        else:
            calls[what](j, k)
    loss[0] = jnp.sum(errors()) / (R * K)
    wire.flush()


def distill(x, st, gate, up, down, gain, proj):
    B, K = x.shape
    N = gate.shape[0]
    S, F = st.shape[1], proj.shape[0]
    T = 16
    R = T * B
    pad, fpad = -(-N // 128) * 128, -(-F // 128) * 128
    teacher, student, downs, grads = plan(K, S, F)
    V = pltpu.VMEM
    D = pltpu.SemaphoreType.DMA
    widest = max(n for _, n, _ in teacher)
    xa = [gather_scratch(n) for _, n, _ in teacher]
    xs = [gather_scratch(n) for _, n, _ in student]
    rs = [reduce_scratch(order, r, R) for _, r, order in downs]
    qs = [reduce_scratch(order, B, n) for _, n, order in grads]
    scratch = [
        [b[0] for b, _ in xa], [s for _, s in xa],
        [b[0] for b, _ in xs], [s for _, s in xs],
        [b for b, _ in rs], [s for _, s in rs],
        [b for b, _ in qs],
        {j: V((4, 2, 2, r, R), bf16) for j, (_, r, _) in enumerate(downs) if not (j < len(teacher) and (B, R) == (r, teacher[j][1]))},
        [V((16 * r, pad), bf16) for _, r, _ in downs],
        V((3, F, R), f32), V((pad, R), bf16), V((2, 2, N, widest), bf16), V((2, pad, TURN), bf16),
        V((F, R), f32), V((F, R), f32), V((F, 128), f32), V((F, R), f32),
        V((fpad, S), bf16), V((K,), bf16), V((fpad, R), bf16), V((R, fpad), bf16),
        V((1, R), f32), V((T, 1, R), f32), V((1, R), f32), V((T, 1, R), f32),
        D((2, 2)), D((2,)), D(()), D(()), D(()), D(()), D(()), D(()),
    ]
    flat, _ = jax.tree.flatten(scratch, is_leaf=lambda s: not isinstance(s, (list, dict)))
    shapes = jax.tree.structure(scratch, is_leaf=lambda s: not isinstance(s, (list, dict)))
    hbm = pl.BlockSpec(memory_space=pl.ANY)
    return pl.pallas_call(
        functools.partial(body, (K, N, S, F, pad, fpad), shapes),
        out_shape=[
            jax.ShapeDtypeStruct((F, S), f32),
            jax.ShapeDtypeStruct((B, S), bf16),
            jax.ShapeDtypeStruct((1,), f32),
        ],
        in_specs=[hbm] * 7,
        out_specs=[
            pl.BlockSpec(memory_space=pltpu.VMEM),
            pl.BlockSpec(memory_space=pltpu.VMEM),
            pl.BlockSpec(memory_space=pltpu.SMEM),
        ],
        scratch_shapes=flat,
        name="distill",
        cost_estimate=pl.CostEstimate(
            flops=6 * R * K * N + 6 * R * S * F,
            bytes_accessed=6 * K * N + 6 * S * F,
            transcendentals=0,
        ),
        compiler_params=pltpu.CompilerParams(
            collective_id=1, has_side_effects=True, vmem_limit_bytes=VMEM_LIMIT
        ),
    )(x, st, gate, up, down, gain, proj)


def local(teacher_in, gate_weight, up_weight, down_weight, post_gain, student_in, proj_weight):
    width_count = lax.axis_size("tensor")
    K, S, F = teacher_in.shape[1], student_in.shape[1], proj_weight.shape[0]
    fits = (
        width_count == 16
        and teacher_in.shape[0] == 32
        and gate_weight.shape[0] == 4 * F
        and S == 5 * 32 * width_count
        and K == width_count * F
        and K % TURN == 0
        and None not in plan(K, S, F)
    )
    if fits:
        proj_grad, student_grad, loss_value = distill(
            teacher_in, student_in, gate_weight, up_weight, down_weight, post_gain, proj_weight
        )
        return loss_value, proj_grad, student_grad
    contract_last = (((1,), (1,)), ((), ()))
    block_rows = lax.all_gather(teacher_in, "tensor", axis=0, tiled=True)
    gate_value = lax.dot_general(
        block_rows, gate_weight, contract_last, preferred_element_type=jnp.float32
    )
    lift_value = lax.dot_general(
        block_rows, up_weight, contract_last, preferred_element_type=jnp.float32
    )
    hidden = (jax.nn.gelu(gate_value, approximate=True) * lift_value).astype(jnp.bfloat16)
    student_all = lax.all_gather(student_in, "tensor", axis=0, tiled=True)
    ffn_out = lax.psum_scatter(
        jnp.dot(hidden, down_weight, preferred_element_type=jnp.float32),
        "tensor",
        scatter_dimension=0,
        tiled=True,
    )
    inv_norm = lax.rsqrt(jnp.mean(ffn_out * ffn_out, axis=-1, keepdims=True) + epsilon)
    target_rows = (
        teacher_in.astype(jnp.float32) + ffn_out * inv_norm * post_gain.astype(jnp.float32)
    ).astype(jnp.bfloat16)
    target = lax.all_to_all(target_rows, "tensor", split_axis=1, concat_axis=0, tiled=True)
    projected = lax.dot_general(
        student_all, proj_weight, contract_last, preferred_element_type=jnp.float32
    )
    difference = projected - target.astype(jnp.float32)
    squares = jnp.sum(difference * difference)
    cotangent = difference.astype(jnp.bfloat16)
    proj_grad = lax.dot_general(
        cotangent, student_all, (((0,), (0,)), ((), ())), preferred_element_type=jnp.float32
    )
    total_error = lax.psum(squares, "tensor")
    student_grad = lax.psum_scatter(
        jnp.dot(cotangent, proj_weight, preferred_element_type=jnp.float32),
        "tensor",
        scatter_dimension=0,
        tiled=True,
    ).astype(jnp.bfloat16)
    loss_value = total_error / (student_all.shape[0] * proj_weight.shape[0] * width_count)
    return (jnp.reshape(loss_value, (1,)), proj_grad, student_grad)


def solution(mesh):
    placed = (
        P(("groups", "tensor"), None),
        P("tensor", None),
        P("tensor", None),
        P("tensor", None),
        P(),
        P(("groups", "tensor"), None),
        P("tensor", None),
    )
    return jax.shard_map(
        local,
        mesh=mesh,
        in_specs=placed,
        out_specs=(P("groups"), P(("groups", "tensor"), None), P(("groups", "tensor"), None)),
        check_vma=False,
    )
```

```python
import functools

import jax
import jax.numpy as jnp
from jax import lax
from jax.experimental import pallas as pl
from jax.experimental.pallas import tpu as pltpu
from jax.sharding import PartitionSpec as P

epsilon = 1e-06
MESH = pl.DeviceIdType.MESH
f32 = jnp.float32
bf16 = jnp.bfloat16
by_last = (((1,), (1,)), ((), ()))

TEACHER = [(512, 'A'), (512, 'A'), (512, 'A'), (512, 'B'), (512, 'A'), (512, 'A'), (512, 'A'), (512, 'A'), (512, 'B'), (512, 'A'), (256, 'A')]
STUDENT = [(640, 'B'), (640, 'B'), (640, 'B'), (640, 'B')]
DOWN = [(32, 'A'), (32, 'B'), (32, 'A'), (32, 'B'), (32, 'A'), (32, 'A'), (32, 'A'), (32, 'A'), (32, 'A'), (32, 'A'), (16, 'A')]
GRAD = [(256, 'A'), (256, 'B'), (256, 'A'), (256, 'A'), (256, 'A'), (256, 'A'), (256, 'B'), (256, 'A'), (256, 'A'), (256, 'A')]
ORDER = [
    ("t", 0, 0), ("t", 1, 0), ("t", 2, 0), ("t", 3, 0), ("t", 4, 0), ("turn", 0, 0), ("turn", 1, 0),
    ("turn", 2, 0), ("turn", 3, 0), ("turn", 4, 0), ("t", 0, 1), ("t", 0, 2), ("turn", 5, 0), ("t", 1, 1),
    ("t", 1, 2), ("turn", 6, 0), ("t", 2, 1), ("t", 2, 2), ("turn", 7, 0), ("turn", 8, 0), ("t", 3, 1),
    ("t", 4, 1), ("t", 4, 2), ("turn", 9, 0), ("t", 0, 3), ("turn", 10, 0), ("turn", 11, 0), ("t", 1, 3),
    ("turn", 12, 0), ("t", 2, 3), ("turn", 13, 0), ("t", 3, 2), ("t", 3, 3), ("t", 5, 0), ("t", 4, 3),
    ("t", 0, 4), ("t", 1, 4), ("t", 2, 4), ("t", 6, 0), ("t", 3, 4), ("t", 0, 5), ("t", 7, 0), ("t", 1, 5),
    ("t", 5, 1), ("t", 5, 2), ("t", 2, 5), ("t", 4, 4), ("t", 0, 6), ("mul", 0, 0), ("t", 6, 1), ("t", 6, 2),
    ("mul", 0, 1), ("t", 1, 6), ("mul", 0, 2), ("t", 2, 6), ("t", 8, 0), ("mul", 0, 3), ("t", 3, 5),
    ("t", 9, 0), ("t", 4, 5), ("t", 7, 1), ("t", 7, 2), ("mul", 1, 0), ("mul", 1, 1), ("t", 5, 3),
    ("mul", 1, 2), ("t", 6, 3), ("t", 3, 6), ("mul", 1, 3), ("t", 4, 6), ("t", 9, 1), ("t", 9, 2),
    ("mul", 2, 0), ("t", 7, 3), ("t", 8, 1), ("mul", 2, 1), ("t", 5, 4), ("mul", 2, 2), ("t", 6, 4),
    ("mul", 2, 3), ("mul", 3, 0), ("t", 9, 3), ("mul", 3, 1), ("t", 7, 4), ("mul", 3, 2), ("t", 5, 5),
    ("t", 8, 2), ("t", 8, 3), ("mul", 3, 3), ("t", 6, 5), ("t", 10, 0), ("mul", 4, 0), ("t", 9, 4),
    ("mul", 4, 1), ("t", 5, 6), ("mul", 4, 2), ("t", 6, 6), ("t", 7, 5), ("mul", 4, 3), ("t", 8, 4),
    ("mul", 5, 0), ("t", 9, 5), ("t", 10, 1), ("t", 10, 2), ("mul", 5, 1), ("t", 7, 6), ("mul", 5, 2),
    ("mul", 5, 3), ("t", 9, 6), ("mul", 6, 0), ("t", 8, 5), ("mul", 6, 1), ("t", 10, 3), ("mul", 6, 2),
    ("mul", 6, 3), ("mul", 7, 0), ("t", 8, 6), ("mul", 7, 1), ("t", 10, 4), ("s", 0, 0), ("s", 1, 0),
    ("mul", 7, 2), ("mul", 7, 3), ("s", 2, 0), ("mul", 8, 0), ("t", 10, 5), ("s", 3, 0), ("mul", 8, 1),
    ("mul", 8, 2), ("s", 0, 1), ("mul", 8, 3), ("t", 10, 6), ("s", 1, 1), ("mul", 9, 0), ("mul", 9, 1),
    ("s", 2, 1), ("mul", 9, 2), ("mul", 9, 3), ("s", 3, 1), ("mul", 10, 0), ("s", 0, 2), ("s", 0, 3),
    ("mul", 10, 1), ("mul", 10, 2), ("mul", 10, 3), ("s", 1, 2), ("s", 1, 3), ("d", 0, 0), ("s", 2, 2),
    ("s", 2, 3), ("d", 1, 0), ("d", 2, 0), ("d", 0, 1), ("s", 3, 2), ("s", 3, 3), ("d", 3, 0), ("d", 1, 1),
    ("s", 0, 4), ("d", 4, 0), ("d", 2, 1), ("d", 5, 0), ("d", 3, 1), ("s", 1, 4), ("d", 6, 0), ("d", 0, 2),
    ("d", 4, 1), ("s", 2, 4), ("d", 7, 0), ("d", 5, 1), ("d", 8, 0), ("d", 1, 2), ("d", 2, 2), ("d", 6, 1),
    ("d", 7, 1), ("s", 3, 4), ("d", 9, 0), ("d", 8, 1), ("s", 0, 5), ("d", 10, 0), ("s", 1, 5), ("d", 4, 2),
    ("d", 9, 1), ("d", 3, 2), ("d", 1, 3), ("s", 0, 6), ("project", 0, 0), ("d", 10, 1), ("s", 2, 5),
    ("s", 1, 6), ("project", 1, 0), ("d", 5, 2), ("d", 0, 3), ("s", 3, 5), ("s", 2, 6), ("project", 2, 0),
    ("d", 1, 4), ("d", 2, 3), ("d", 3, 3), ("d", 6, 2), ("s", 3, 6), ("project", 3, 0), ("d", 0, 4),
    ("d", 4, 3), ("d", 2, 4), ("d", 5, 3), ("d", 4, 4), ("d", 6, 3), ("d", 5, 4), ("d", 7, 2), ("d", 3, 4),
    ("d", 0, 5), ("d", 7, 3), ("d", 6, 4), ("d", 2, 5), ("d", 8, 2), ("d", 8, 3), ("d", 7, 4), ("d", 4, 5),
    ("d", 9, 2), ("d", 5, 5), ("d", 10, 2), ("d", 1, 5), ("d", 3, 5), ("d", 6, 5), ("d", 9, 3), ("d", 8, 4),
    ("d", 10, 3), ("d", 9, 4), ("d", 10, 4), ("d", 7, 5), ("d", 8, 5), ("d", 9, 5), ("d", 10, 5),
    ("norm", 0, 0), ("g", 0, 0), ("g", 1, 0), ("g", 2, 0), ("loss", 0, 0), ("g", 3, 0), ("g", 4, 0),
    ("g", 5, 0), ("g", 6, 0), ("g", 0, 1), ("g", 7, 0), ("g", 1, 1), ("g", 2, 1), ("g", 8, 0), ("g", 3, 1),
    ("g", 4, 1), ("g", 9, 0), ("g", 5, 1), ("g", 6, 1), ("pg", 0, 0), ("g", 7, 1), ("g", 8, 1), ("pg", 1, 0),
    ("g", 9, 1), ("g", 0, 2), ("pg", 2, 0), ("pg", 3, 0), ("g", 2, 2), ("g", 1, 2), ("g", 3, 2), ("g", 4, 2),
    ("g", 6, 2), ("g", 1, 3), ("g", 0, 3), ("g", 2, 3), ("g", 6, 3), ("g", 3, 3), ("g", 0, 4), ("g", 4, 3),
    ("g", 2, 4), ("g", 3, 4), ("g", 4, 4), ("g", 5, 2), ("g", 5, 3), ("g", 1, 4), ("g", 7, 2), ("g", 7, 3),
    ("g", 8, 2), ("g", 6, 4), ("g", 0, 5), ("g", 2, 5), ("g", 9, 2), ("g", 3, 5), ("g", 8, 3), ("g", 1, 5),
    ("g", 5, 4), ("g", 6, 5), ("g", 9, 3), ("g", 7, 4), ("g", 8, 4), ("g", 4, 5), ("g", 9, 4), ("g", 5, 5),
    ("g", 7, 5), ("g", 8, 5), ("g", 9, 5),
]
TURN = 384
VMEM_LIMIT = 58 * 2**20


class Place:
    def __init__(self):
        self.me = me = lax.axis_index("tensor")
        self.c = c = lax.rem(me, 2)
        self.y = y = lax.rem(me // 2, 2)
        self.z = z = me // 4
        self.low = z // 2
        odd = lax.rem(z, 2)
        self.mid = (z == 1) | (z == 2)
        self.end = (z == 0) | (z == 3)
        self.core = me + 1 - 2 * c
        self.across = me + 2 - 4 * y
        self.near_z = z + 1 - 2 * odd
        self.far_z = 3 - z
        self.other_mid = 2 - self.low
        self.other_end = 3 - 3 * self.low
        self.near = self.near_z * 4 + y * 2 + c
        self.far = self.far_z * 4 + y * 2 + c


class Wire:
    def __init__(self):
        self.owed = []

    def make(self, src, dst, send_sem, recv_sem, target):
        return pltpu.make_async_remote_copy(
            src_ref=src, dst_ref=dst, send_sem=send_sem, recv_sem=recv_sem,
            device_id={"tensor": target}, device_id_type=MESH,
        )

    def send(self, src, dst, send_sem, recv_sem, target, when=None):
        copy = self.make(src, dst, send_sem, recv_sem, target)
        if when is None:
            copy.start()
        else:
            pl.when(when)(copy.start)

    def arrived(self, like, recv_sem, target):
        self.make(like, like, recv_sem, recv_sem, target).wait_recv()

    def owe(self, like, send_sem, target, when=None):
        self.owed.append((when, self.make(like, like, send_sem, send_sem, target)))

    def flush(self):
        for when, copy in self.owed:
            if when is None:
                copy.wait_send()
            else:
                pl.when(when)(copy.wait_send)
        self.owed = []


class Gather:
    ops = 7

    def __init__(self, at, wire, order, own, buf, sems):
        self.at, self.wire, self.order, self.own, self.buf = at, wire, order, own, buf
        self.zn, self.zf, self.ys, self.yr, self.cs, self.cr, self.ls = (sems.at[i] for i in range(7))
        self.zr = [sems.at[7 + i] for i in range(3)]

    def row(self, z):
        if self.order == "A":
            return self.buf.at[z, self.at.y, self.at.c]
        return self.buf.at[z, :, self.at.c]

    def z_copy(self, z, land, target, src=None):
        row = self.row(z)
        sem = self.zn if target is self.at.near else self.zf
        return self.wire.make(row if src is None else src, row, sem, self.zr[land], target)

    def z_wait(self, z, land):
        self.wire.arrived(self.row(z), self.zr[land], self.at.near)

    def y_copy(self, z, src=None):
        at = self.at
        row = self.buf.at[z, at.y, at.c]
        return self.wire.make(row if src is None else src, row, self.ys, self.yr, at.across)

    def c_send(self, part):
        self.wire.send(part, part, self.cs, self.cr, self.at.core)

    def keep(self):
        at = self.at
        return pltpu.make_async_copy(self.own, self.buf.at[at.z, at.y, at.c], self.ls)

    def debts(self):
        at, buf, owe = self.at, self.buf, self.wire.owe
        owe(buf.at[:, at.y, at.c] if self.order == "A" else buf.at[at.z, at.y, at.c], self.ys, at.across)
        owe(buf.at[:, :, at.c], self.cs, at.core)
        owe(self.row(at.z), self.zn, at.near, when=at.end)
        owe(self.row(pl.ds(0, 3)), self.zn, at.near, when=at.mid)
        owe(self.row(pl.ds(0, 2)), self.zf, at.far, when=at.mid)

    def op(self, k):
        at = self.at
        if self.order == "A":
            self.op_a(k, at)
        else:
            self.op_b(k, at)
        if k == 6:
            self.debts()

    def pass_on(self, who, z, land, target=None, there=None):
        copies = []
        if target is not None:
            copies.append(self.z_copy(z, there, target))
        if self.order == "A":
            copies.append(self.y_copy(z))

        @pl.when(who)
        def _():
            self.z_wait(z, land)
            for copy in copies:
                copy.start()

    def op_a(self, k, at):
        buf = self.buf
        if k == 0:
            self.z_copy(at.z, 0, at.near, src=self.own).start()
            pl.when(at.mid)(self.z_copy(at.z, 1, at.far, src=self.own).start)
            self.y_copy(at.z, src=self.own).start()
            self.keep().start()
        elif k == 1:
            self.z_wait(at.near_z, 0)
            pl.when(at.mid)(self.z_copy(at.near_z, 2, at.far).start)
            self.y_copy(at.near_z).start()
        elif k == 2:
            self.pass_on(at.mid, at.other_mid, 1, at.near, 1)
        elif k == 3:
            self.pass_on(at.mid, at.other_end, 2, at.near, 2)
            self.pass_on(at.end, at.other_mid, 1)
        elif k == 4:
            self.pass_on(at.end, at.other_end, 2)
            self.keep().wait()
            self.c_send(buf.at[:, at.y, at.c])
        elif k == 5:
            self.wire.arrived(buf.at[:, 1 - at.y, at.c], self.yr, at.across)
            self.c_send(buf.at[:, 1 - at.y, at.c])
        else:
            self.wire.arrived(buf.at[:, :, 1 - at.c], self.cr, at.core)

    def op_b(self, k, at):
        buf = self.buf
        if k == 0:
            self.y_copy(at.z, src=self.own).start()
            self.keep().start()
        elif k == 1:
            self.keep().wait()
            self.wire.arrived(buf.at[at.z, 1 - at.y, at.c], self.yr, at.across)
            self.z_copy(at.z, 0, at.near).start()
            pl.when(at.mid)(self.z_copy(at.z, 1, at.far).start)
        elif k == 2:
            self.pass_on(at.mid, at.near_z, 0, at.far, 2)
        elif k == 3:
            self.pass_on(at.mid, at.other_mid, 1, at.near, 1)
        elif k == 4:
            self.pass_on(at.mid, at.other_end, 2, at.near, 2)
        elif k == 5:

            @pl.when(at.end)
            def _():
                self.z_wait(at.near_z, 0)
                self.z_wait(at.other_mid, 1)
                self.z_wait(at.other_end, 2)

            self.c_send(buf.at[:, :, at.c])
        else:
            self.wire.arrived(buf.at[:, :, 1 - at.c], self.cr, at.core)


class Reduce:
    ops = 6

    def __init__(self, at, wire, order, part, fill, finish, bufs, sems):
        self.at, self.wire, self.order = at, wire, order
        self.part, self.fill, self.finish = part, fill, finish
        self.r1, self.s1, self.yb, self.r2, self.go, self.rn, self.rf = bufs
        self.cs, self.ys, self.yr, self.ns, self.nr, self.fs, self.fr = (sems.at[i] for i in range(7))
        self.cr = [sems.at[7 + i] for i in range(2)]

    def debts(self):
        at, owe = self.at, self.wire.owe
        owe(self.r1, self.cs, at.core)
        owe(self.s1 if self.order == "A" else self.yb, self.ys, at.across)
        owe(self.go, self.ns, at.near, when=at.end)
        owe(self.go.at[pl.ds(2, 1)], self.ns, at.near, when=at.mid)
        owe(self.go.at[pl.ds(0, 2)], self.fs, at.far, when=at.mid)

    def op(self, k):
        at = self.at
        if k == 0:
            self.begin(at)
        elif self.order == "A":
            self.op_a(k, at)
        else:
            self.op_b(k, at)
        if k == 5:
            self.debts()

    def begin(self, at):
        self.fill()
        for i, y in enumerate((1 - at.y, at.y)):
            self.wire.send(self.part(y, 1 - at.c), self.r1.at[y], self.cs, self.cr[i], at.core)

    def c_wait(self, at, i):
        y = (1 - at.y, at.y)[i]
        self.wire.arrived(self.r1.at[y], self.cr[i], at.core)

    def two(self, y, zs):
        at = self.at
        return self.part(y, at.c)[zs].astype(f32) + self.r1[y, zs].astype(f32)

    def total(self, zs):
        at = self.at
        if self.order == "A":
            return self.two(at.y, zs) + self.r2[zs].astype(f32)
        return jnp.stack([self.two(y, zs) for y in range(2)], axis=1)

    def z_ops(self, k, at):
        go, rn, rf = self.go, self.rn, self.rf
        if k == 0:
            inward = self.wire.make(go, rn, self.ns, self.nr, at.near)

            @pl.when(at.end)
            def _():
                go[...] = self.total(pl.ds(1 - at.low, 3)).astype(bf16)
                inward.start()

        elif k == 1:
            onward = self.wire.make(go.at[pl.ds(0, 2)], rf, self.fs, self.fr, at.far)

            @pl.when(at.mid)
            def _():
                self.wire.arrived(rn, self.nr, at.near)
                there = self.total(pl.ds(2 - 2 * at.low, 2))
                go[0:2] = (there + rn[pl.ds(1 - at.low, 2)].astype(f32)).astype(bf16)
                onward.start()

        elif k == 2:
            back = self.wire.make(go.at[pl.ds(2, 1)], rn.at[pl.ds(0, 1)], self.ns, self.nr, at.near)

            @pl.when(at.mid)
            def _():
                self.wire.arrived(rf, self.fr, at.far)
                there = self.total(pl.ds(at.near_z, 1))
                go[2:3] = (there + rf[pl.ds(at.low, 1)].astype(f32)).astype(bf16)
                back.start()

    def own(self, at, done):
        rn, rf = self.rn, self.rf

        @pl.when(at.end)
        def _():
            self.wire.arrived(rn.at[pl.ds(0, 1)], self.nr, at.near)
            done((self.total(pl.ds(at.z, 1)) + rn[0:1].astype(f32))[0])

        @pl.when(at.mid)
        def _():
            done(
                (
                    self.total(pl.ds(at.z, 1))
                    + rn[pl.ds(2 * at.low, 1)].astype(f32)
                    + rf[pl.ds(1 - at.low, 1)].astype(f32)
                )[0]
            )

    def op_a(self, k, at):
        every = pl.ds(0, 4)
        if k == 1:
            self.c_wait(at, 0)
            self.s1[...] = self.two(1 - at.y, every).astype(bf16)
            self.wire.send(self.s1, self.r2, self.ys, self.yr, at.across)
        elif k == 2:
            self.c_wait(at, 1)
            self.wire.arrived(self.r2, self.yr, at.across)
            self.z_ops(0, at)
        elif k == 3:
            self.z_ops(1, at)
        elif k == 4:
            self.z_ops(2, at)
        else:
            self.own(at, self.finish)

    def op_b(self, k, at):
        if k == 1:
            self.c_wait(at, 0)
            self.c_wait(at, 1)
            self.z_ops(0, at)
        elif k == 2:
            self.z_ops(1, at)
        elif k == 3:
            self.z_ops(2, at)
        elif k == 4:

            def store(v):
                self.s1[...] = v

            self.own(at, store)
            self.yb[...] = self.s1[1 - at.y].astype(bf16)
            self.wire.send(self.yb, self.r2, self.ys, self.yr, at.across)
        else:
            self.wire.arrived(self.r2, self.yr, at.across)
            self.finish(self.s1[at.y] + self.r2[...].astype(f32))


def reduce_scratch(order, r, n):
    V = pltpu.VMEM
    D = pltpu.SemaphoreType.DMA
    two = () if order == "A" else (2,)
    bufs = [
        V((2, 4, r, n), bf16),
        V((4, r, n), bf16) if order == "A" else V((2, r, n), f32),
        V((16, 128) if order == "A" else (r, n), bf16),
        V((4, r, n), bf16) if order == "A" else V((r, n), bf16),
        V((3,) + two + (r, n), bf16), V((3,) + two + (r, n), bf16), V((2,) + two + (r, n), bf16),
    ]
    return bufs, D((9,))


def gather_scratch(n):
    D = pltpu.SemaphoreType.DMA
    return [pltpu.VMEM((4, 2, 2, 32, n), bf16)], D((10,))


def cut(pieces, whole):
    starts, at = [], 0
    for size, order in pieces:
        starts.append((at, size, order))
        at += size
    return starts if at == whole else None


def plan(K, S, F):
    return cut(TEACHER, K), cut(STUDENT, S), cut(DOWN, F), cut(GRAD, S)


def body(dims, shapes, *refs):
    x, st, gate, up, down, gain, proj, pg, sg, loss = refs[:10]
    take = iter(jax.tree.unflatten(shapes, refs[10:]))
    K, N, S, F, pad, fpad = dims
    teacher, student, downs, grads = plan(K, S, F)
    xa, xsems, xs, ssems, rbuf, rsem, qbuf, parts, wt = (next(take) for _ in range(9))
    (acc, hidden, wbuf, dbuf, ffn, base, gcol, projected, pbuf, gbuf, cot_t, cot,
     nb, nr, lb, lr, wsem, dsem, psem, gsem, ns_, nr_, ls_, lr_) = take
    at, wire = Place(), Wire()
    B = x.shape[0]
    T = 16
    R = T * B
    half = N // 2
    turns = K // TURN
    me = at.me

    def fetch(j):
        first, n, _ = teacher[j]
        return [
            pltpu.make_async_copy(
                w.at[:, pl.ds(first, n)], wbuf.at[i, j % 2, :, pl.ds(0, n)], wsem.at[i, j % 2]
            )
            for i, w in enumerate((gate, up))
        ]

    def fetch_down(i):
        return pltpu.make_async_copy(
            down.at[:, pl.ds(i * TURN, TURN)], dbuf.at[i % 2, pl.ds(0, N)], dsem.at[i % 2]
        )

    projector = pltpu.make_async_copy(proj, pbuf.at[pl.ds(0, F)], psem)
    gains = pltpu.make_async_copy(gain, gbuf, gsem)

    for j in range(2):
        for copy in fetch(j):
            copy.start()
        fetch_down(j).start()
    projector.start()
    gains.start()
    others = [lax.rem(me + k, T) for k in range(1, T)]
    barrier = pltpu.get_barrier_semaphore()
    for target in others:
        pl.semaphore_signal(barrier, inc=1, device_id={"tensor": target}, device_id_type=MESH)
    pl.semaphore_wait(barrier, T - 1)

    gathers = [
        Gather(at, Wire(), order, x.at[:, pl.ds(first, n)], xa[j], xsems[j])
        for j, (first, n, order) in enumerate(teacher)
    ] + [
        Gather(at, wire, order, st.at[:, pl.ds(first, n)], xs[j], ssems[j])
        for j, (first, n, order) in enumerate(student)
    ]

    def clear():
        dbuf[:, N:pad] = jnp.zeros((2, pad - N, TURN), bf16)
        hidden[N:pad] = jnp.zeros((pad - N, R), bf16)
        pbuf[F:fpad] = jnp.zeros((fpad - F, S), bf16)
        cot_t[F:fpad] = jnp.zeros((fpad - F, R), bf16)
        base[...] = jnp.zeros_like(base)
        gcol[...] = jnp.zeros_like(gcol)

    def held(which, part):
        q = which * 4 + part
        return pg.at[:, pl.ds(q * R, R)] if q < 5 else acc.at[q - 5]

    def multiply(j, i):
        first, n, _ = teacher[j]
        which, side = i % 2, i // 2
        if i == 0:
            for copy in fetch(j):
                copy.wait()

        @pl.loop(0, 1)
        def _(_):
            d = lax.dot_general(
                wbuf[which, j % 2, side * half : (side + 1) * half, 0:n], xa[j][...].reshape(R, n),
                by_last, preferred_element_type=f32,
            )
            for q in range(2):
                part = d[q * F : (q + 1) * F]
                place = held(which, side * 2 + q)
                if j > 0:
                    part += place[...]
                if j < len(teacher) - 1 or which == 0:
                    place[...] = part
                else:
                    rows = slice(side * half + q * F, side * half + (q + 1) * F)
                    value = held(0, side * 2 + q)[...]
                    hidden[rows] = (jax.nn.gelu(value, approximate=True) * part).astype(bf16)

        if i == 3:
            own_part(j)
            if j + 2 < len(teacher):
                for copy in fetch(j + 2):
                    copy.start()

    def one(rows, cols, off):
        i = lax.broadcasted_iota(jnp.int32, (rows, cols), 0)
        k = lax.broadcasted_iota(jnp.int32, (rows, cols), 1)
        return jnp.where(i == k + off, 1.0, 0.0).astype(bf16)

    def turn(i):
        fetch_down(i).wait()
        got = dbuf[i % 2].T
        row = 0
        while row < TURN:
            d, r = divmod(i * TURN + row, F)
            j = max(q for q, (first, _, _) in enumerate(downs) if first <= r)
            first, size, _ = downs[j]
            run = min(TURN - row, first + size - r)
            begin = d * size + r - first
            wt[j][begin : begin + run] = got[row : row + run]
            row += run
        if i + 2 < turns:
            fetch_down(i + 2).start()

    def own_part(j):
        first, n, _ = teacher[j]

        @pl.when((first < F * me + F) & (first + n > F * me))
        def _():
            sel = one(F, n, first - F * me)
            base[...] += lax.dot_general(
                sel, xa[j][...].reshape(R, n), by_last, preferred_element_type=f32
            )
            wide = jnp.broadcast_to(gbuf[first : first + n][None], (128, n))
            gcol[...] += lax.dot_general(sel, wide, by_last, preferred_element_type=f32)

    def project(j):
        first, n, _ = student[j]
        got = lax.dot_general(
            pbuf[0:F, first : first + n], xs[j][...].reshape(R, n), by_last,
            preferred_element_type=f32,
        )
        projected[...] = got if j == 0 else projected[...] + got

    def down_item(j):
        first, r, order = downs[j]

        held_by = parts[j] if j in parts else xa[j]

        def fill():
            if j not in parts:
                gathers[j].wire.flush()

            @pl.loop(0, 1)
            def _(_):
                got = jnp.dot(wt[j][...], hidden[...], preferred_element_type=f32)
                held_by[...] = got.astype(bf16).reshape(4, 2, 2, r, R)

        def finish(v):
            ffn[first : first + r] = v

        return Reduce(at, wire, order, lambda y, c: held_by.at[:, y, c], fill, finish, rbuf[j], rsem[j])

    def grad_item(j):
        first, n, order = grads[j]

        def fill():
            @pl.loop(0, 1)
            def _(_):
                got = jnp.dot(cot[...], pbuf[:, first : first + n], preferred_element_type=f32)
                xa[j][:, :, :, :, 0:n] = got.astype(bf16).reshape(4, 2, 2, B, n)

        def finish(v):
            sg[:, first : first + n] = v.astype(bf16)

        return Reduce(
            at, wire, order, lambda y, c: xa[j].at[:, y, c, :, pl.ds(0, n)], fill, finish,
            qbuf[j], rsem[j],
        )

    down_items = [down_item(j) for j in range(len(downs))]
    grad_items = [grad_item(j) for j in range(len(grads))]

    def everyone(src, dst, ss, rs):
        for v in others:
            wire.send(src, dst.at[me], ss, rs, v)
        dst[me] = src[...]
        wire.owe(dst.at[pl.ds(0, T - 1)], ss, others[0])

        def collect():
            wire.arrived(dst.at[pl.ds(0, T - 1)], rs, others[0])
            return jnp.sum(dst[...], axis=0)

        return collect

    def norm():
        whole = ffn[...]
        nb[...] = jnp.sum(whole * whole, axis=0, keepdims=True)
        collect = everyone(nb, nr, ns_, nr_)
        for gather in gathers:
            gather.wire.flush()
        wire.flush()
        inv_norm = lax.rsqrt(collect() / K + epsilon)
        target = (base[...] + ffn[...] * inv_norm * gcol[:, 0:1]).astype(bf16)
        difference = projected[...] - target.astype(f32)
        cot_t[0:F] = difference.astype(bf16)
        cot[...] = cot_t[...].T
        lb[...] = jnp.sum(difference * difference, axis=0, keepdims=True)

    def proj_grad(j):
        first, n, _ = student[j]
        pg[:, first : first + n] = jnp.dot(
            cot_t[0:F], xs[j][...].reshape(R, n), preferred_element_type=f32
        )

    calls = {
        "t": lambda j, k: gathers[j].op(k),
        "s": lambda j, k: gathers[len(teacher) + j].op(k),
        "d": lambda j, k: down_items[j].op(k),
        "g": lambda j, k: grad_items[j].op(k),
        "mul": multiply,
        "turn": lambda j, k: turn(j),
        "project": lambda j, k: project(j),
        "pg": lambda j, k: proj_grad(j),
    }
    started = False
    for what, j, k in ORDER:
        if what not in ("t", "s") and not started:
            started = True
            clear()
            projector.wait()
            gains.wait()
        if what == "norm":
            norm()
        elif what == "loss":
            errors = everyone(lb, lr, ls_, lr_)
        else:
            calls[what](j, k)
    loss[...] = jnp.broadcast_to(jnp.sum(errors(), axis=1, keepdims=True) / (R * K), loss.shape)
    wire.flush()


def distill(x, st, gate, up, down, gain, proj):
    B, K = x.shape
    N = gate.shape[0]
    S, F = st.shape[1], proj.shape[0]
    T = 16
    R = T * B
    pad, fpad = -(-N // 128) * 128, -(-F // 128) * 128
    teacher, student, downs, grads = plan(K, S, F)
    V = pltpu.VMEM
    D = pltpu.SemaphoreType.DMA
    widest = max(n for _, n, _ in teacher)
    xa = [gather_scratch(n) for _, n, _ in teacher]
    xs = [gather_scratch(n) for _, n, _ in student]
    rs = [reduce_scratch(order, r, R) for _, r, order in downs]
    qs = [reduce_scratch(order, B, n) for _, n, order in grads]
    scratch = [
        [b[0] for b, _ in xa], [s for _, s in xa],
        [b[0] for b, _ in xs], [s for _, s in xs],
        [b for b, _ in rs], [s for _, s in rs],
        [b for b, _ in qs],
        {j: V((4, 2, 2, r, R), bf16) for j, (_, r, _) in enumerate(downs) if not (j < len(teacher) and (B, R) == (r, teacher[j][1]))},
        [V((16 * r, pad), bf16) for _, r, _ in downs],
        V((3, F, R), f32), V((pad, R), bf16), V((2, 2, N, widest), bf16), V((2, pad, TURN), bf16),
        V((F, R), f32), V((F, R), f32), V((F, 128), f32), V((F, R), f32),
        V((fpad, S), bf16), V((K,), bf16), V((fpad, R), bf16), V((R, fpad), bf16),
        V((1, R), f32), V((T, 1, R), f32), V((1, R), f32), V((T, 1, R), f32),
        D((2, 2)), D((2,)), D(()), D(()), D(()), D(()), D(()), D(()),
    ]
    flat, _ = jax.tree.flatten(scratch, is_leaf=lambda s: not isinstance(s, (list, dict)))
    shapes = jax.tree.structure(scratch, is_leaf=lambda s: not isinstance(s, (list, dict)))
    hbm = pl.BlockSpec(memory_space=pl.ANY)
    return pl.pallas_call(
        functools.partial(body, (K, N, S, F, pad, fpad), shapes),
        out_shape=[
            jax.ShapeDtypeStruct((F, S), f32),
            jax.ShapeDtypeStruct((B, S), bf16),
            jax.ShapeDtypeStruct((8, 128), f32),
        ],
        in_specs=[hbm] * 7,
        out_specs=[
            pl.BlockSpec(memory_space=pltpu.VMEM),
            pl.BlockSpec(memory_space=pltpu.VMEM),
            pl.BlockSpec(memory_space=pltpu.VMEM),
        ],
        scratch_shapes=flat,
        name="distill",
        cost_estimate=pl.CostEstimate(
            flops=6 * R * K * N + 6 * R * S * F,
            bytes_accessed=6 * K * N + 6 * S * F,
            transcendentals=0,
        ),
        compiler_params=pltpu.CompilerParams(
            collective_id=1, has_side_effects=True, vmem_limit_bytes=VMEM_LIMIT
        ),
    )(x, st, gate, up, down, gain, proj)


def local(teacher_in, gate_weight, up_weight, down_weight, post_gain, student_in, proj_weight):
    width_count = lax.axis_size("tensor")
    K, S, F = teacher_in.shape[1], student_in.shape[1], proj_weight.shape[0]
    fits = (
        width_count == 16
        and teacher_in.shape[0] == 32
        and gate_weight.shape[0] == 4 * F
        and S == 5 * 32 * width_count
        and K == width_count * F
        and K % TURN == 0
        and None not in plan(K, S, F)
    )
    if fits:
        proj_grad, student_grad, loss_value = distill(
            teacher_in, student_in, gate_weight, up_weight, down_weight, post_gain, proj_weight
        )
        return loss_value[0:1, 0], proj_grad, student_grad
    contract_last = (((1,), (1,)), ((), ()))
    block_rows = lax.all_gather(teacher_in, "tensor", axis=0, tiled=True)
    gate_value = lax.dot_general(
        block_rows, gate_weight, contract_last, preferred_element_type=jnp.float32
    )
    lift_value = lax.dot_general(
        block_rows, up_weight, contract_last, preferred_element_type=jnp.float32
    )
    hidden = (jax.nn.gelu(gate_value, approximate=True) * lift_value).astype(jnp.bfloat16)
    student_all = lax.all_gather(student_in, "tensor", axis=0, tiled=True)
    ffn_out = lax.psum_scatter(
        jnp.dot(hidden, down_weight, preferred_element_type=jnp.float32),
        "tensor",
        scatter_dimension=0,
        tiled=True,
    )
    inv_norm = lax.rsqrt(jnp.mean(ffn_out * ffn_out, axis=-1, keepdims=True) + epsilon)
    target_rows = (
        teacher_in.astype(jnp.float32) + ffn_out * inv_norm * post_gain.astype(jnp.float32)
    ).astype(jnp.bfloat16)
    target = lax.all_to_all(target_rows, "tensor", split_axis=1, concat_axis=0, tiled=True)
    projected = lax.dot_general(
        student_all, proj_weight, contract_last, preferred_element_type=jnp.float32
    )
    difference = projected - target.astype(jnp.float32)
    squares = jnp.sum(difference * difference)
    cotangent = difference.astype(jnp.bfloat16)
    proj_grad = lax.dot_general(
        cotangent, student_all, (((0,), (0,)), ((), ())), preferred_element_type=jnp.float32
    )
    total_error = lax.psum(squares, "tensor")
    student_grad = lax.psum_scatter(
        jnp.dot(cotangent, proj_weight, preferred_element_type=jnp.float32),
        "tensor",
        scatter_dimension=0,
        tiled=True,
    ).astype(jnp.bfloat16)
    loss_value = total_error / (student_all.shape[0] * proj_weight.shape[0] * width_count)
    return (jnp.reshape(loss_value, (1,)), proj_grad, student_grad)


def solution(mesh):
    placed = (
        P(("groups", "tensor"), None),
        P("tensor", None),
        P("tensor", None),
        P("tensor", None),
        P(),
        P(("groups", "tensor"), None),
        P("tensor", None),
    )
    return jax.shard_map(
        local,
        mesh=mesh,
        in_specs=placed,
        out_specs=(P("groups"), P(("groups", "tensor"), None), P(("groups", "tensor"), None)),
        check_vma=False,
    )
```

```python
import functools

import jax
import jax.numpy as jnp
from jax import lax
from jax.experimental import pallas as pl
from jax.experimental.pallas import tpu as pltpu
from jax.sharding import PartitionSpec as P

epsilon = 1e-06
MESH = pl.DeviceIdType.MESH
f32 = jnp.float32
bf16 = jnp.bfloat16
by_last = (((1,), (1,)), ((), ()))

TEACHER = [(512, 'A'), (512, 'A'), (512, 'B'), (512, 'A'), (512, 'A'), (512, 'A'), (512, 'A'), (512, 'B'), (512, 'A'), (512, 'A'), (256, 'A')]
STUDENT = [(640, 'B'), (640, 'B'), (640, 'B'), (640, 'B')]
DOWN = [(32, 'A'), (32, 'B'), (32, 'A'), (32, 'B'), (32, 'A'), (32, 'A'), (32, 'A'), (32, 'A'), (32, 'A'), (32, 'A'), (16, 'A')]
GRAD = [(256, 'A'), (256, 'B'), (256, 'A'), (256, 'A'), (256, 'A'), (256, 'A'), (256, 'B'), (256, 'A'), (256, 'A'), (256, 'A')]
ORDER = [
    ("t", 0, 0), ("turn", 0, 0), ("t", 1, 0), ("turn", 1, 0), ("t", 2, 0), ("t", 3, 0), ("turn", 2, 0),
    ("t", 4, 0), ("turn", 3, 0), ("turn", 4, 0), ("t", 0, 1), ("t", 0, 2), ("turn", 5, 0), ("t", 1, 1),
    ("t", 1, 2), ("turn", 6, 0), ("t", 3, 1), ("t", 2, 1), ("t", 3, 2), ("turn", 7, 0), ("turn", 8, 0),
    ("t", 4, 1), ("t", 4, 2), ("turn", 9, 0), ("t", 0, 3), ("turn", 10, 0), ("turn", 11, 0), ("t", 1, 3),
    ("t", 2, 2), ("turn", 12, 0), ("turn", 13, 0), ("t", 2, 3), ("t", 5, 0), ("t", 3, 3), ("t", 4, 3),
    ("t", 0, 4), ("t", 1, 4), ("t", 6, 0), ("t", 2, 4), ("t", 7, 0), ("t", 5, 1), ("t", 5, 2), ("t", 3, 4),
    ("t", 0, 5), ("t", 4, 4), ("t", 1, 5), ("t", 6, 1), ("t", 6, 2), ("t", 0, 6), ("mul", 0, 0), ("t", 1, 6),
    ("t", 2, 5), ("t", 3, 5), ("t", 8, 0), ("mul", 0, 1), ("t", 4, 5), ("t", 5, 3), ("mul", 1, 0),
    ("t", 6, 3), ("t", 2, 6), ("t", 7, 1), ("mul", 1, 1), ("t", 3, 6), ("t", 4, 6), ("t", 5, 4),
    ("mul", 2, 0), ("t", 6, 4), ("t", 8, 1), ("t", 8, 2), ("mul", 2, 1), ("t", 9, 0), ("mul", 3, 0),
    ("t", 5, 5), ("t", 10, 0), ("mul", 3, 1), ("t", 6, 5), ("t", 7, 2), ("t", 7, 3), ("t", 8, 3),
    ("mul", 4, 0), ("t", 5, 6), ("mul", 4, 1), ("t", 6, 6), ("t", 9, 1), ("t", 9, 2), ("mul", 5, 0),
    ("t", 8, 4), ("t", 7, 4), ("t", 10, 1), ("t", 10, 2), ("mul", 5, 1), ("mul", 6, 0), ("t", 9, 3),
    ("t", 7, 5), ("mul", 6, 1), ("t", 8, 5), ("t", 10, 3), ("t", 9, 4), ("t", 10, 4), ("s", 0, 0),
    ("s", 1, 0), ("t", 7, 6), ("mul", 7, 0), ("t", 8, 6), ("s", 2, 0), ("mul", 7, 1), ("t", 9, 5),
    ("s", 3, 0), ("t", 10, 5), ("mul", 8, 0), ("mul", 8, 1), ("t", 9, 6), ("s", 0, 1), ("mul", 9, 0),
    ("t", 10, 6), ("s", 1, 1), ("mul", 9, 1), ("s", 2, 1), ("mul", 10, 0), ("s", 3, 1), ("mul", 10, 1),
    ("d", 0, 0), ("s", 0, 2), ("s", 0, 3), ("d", 1, 0), ("s", 1, 2), ("s", 1, 3), ("d", 2, 0), ("d", 0, 1),
    ("d", 3, 0), ("d", 1, 1), ("s", 2, 2), ("s", 2, 3), ("d", 4, 0), ("d", 2, 1), ("s", 3, 2), ("s", 3, 3),
    ("d", 5, 0), ("d", 3, 1), ("s", 0, 4), ("d", 6, 0), ("d", 0, 2), ("d", 4, 1), ("s", 1, 4), ("d", 7, 0),
    ("d", 5, 1), ("s", 2, 4), ("d", 6, 1), ("d", 8, 0), ("d", 2, 2), ("d", 9, 0), ("d", 1, 2), ("d", 7, 1),
    ("s", 0, 5), ("s", 3, 4), ("d", 10, 0), ("d", 8, 1), ("d", 4, 2), ("s", 1, 5), ("d", 9, 1), ("s", 0, 6),
    ("project", 0, 0), ("d", 10, 1), ("d", 3, 2), ("s", 2, 5), ("s", 1, 6), ("project", 1, 0), ("d", 5, 2),
    ("d", 1, 3), ("d", 0, 3), ("s", 3, 5), ("s", 2, 6), ("project", 2, 0), ("d", 1, 4), ("d", 6, 2),
    ("d", 2, 3), ("d", 3, 3), ("s", 3, 6), ("project", 3, 0), ("d", 0, 4), ("d", 4, 3), ("d", 2, 4),
    ("d", 5, 3), ("d", 4, 4), ("d", 6, 3), ("d", 5, 4), ("d", 7, 2), ("d", 3, 4), ("d", 0, 5), ("d", 7, 3),
    ("d", 6, 4), ("d", 2, 5), ("d", 8, 2), ("d", 8, 3), ("d", 7, 4), ("d", 4, 5), ("d", 9, 2), ("d", 5, 5),
    ("d", 10, 2), ("d", 1, 5), ("d", 3, 5), ("d", 6, 5), ("d", 9, 3), ("d", 8, 4), ("d", 10, 3), ("d", 9, 4),
    ("d", 10, 4), ("d", 7, 5), ("d", 8, 5), ("d", 9, 5), ("d", 10, 5), ("norm", 0, 0), ("g", 0, 0),
    ("g", 1, 0), ("g", 2, 0), ("loss", 0, 0), ("g", 3, 0), ("g", 4, 0), ("g", 5, 0), ("g", 6, 0), ("g", 0, 1),
    ("g", 7, 0), ("g", 1, 1), ("g", 2, 1), ("g", 8, 0), ("g", 3, 1), ("g", 4, 1), ("g", 9, 0), ("g", 5, 1),
    ("g", 6, 1), ("g", 7, 1), ("g", 8, 1), ("g", 9, 1), ("g", 0, 2), ("g", 2, 2), ("g", 1, 2), ("g", 3, 2),
    ("g", 4, 2), ("g", 6, 2), ("g", 1, 3), ("g", 0, 3), ("g", 2, 3), ("g", 6, 3), ("g", 3, 3), ("g", 0, 4),
    ("g", 4, 3), ("g", 2, 4), ("g", 3, 4), ("g", 4, 4), ("g", 5, 2), ("g", 5, 3), ("g", 1, 4), ("g", 7, 2),
    ("g", 7, 3), ("g", 8, 2), ("g", 6, 4), ("g", 0, 5), ("g", 2, 5), ("g", 9, 2), ("g", 3, 5), ("g", 8, 3),
    ("g", 1, 5), ("g", 5, 4), ("g", 6, 5), ("g", 9, 3), ("g", 7, 4), ("g", 8, 4), ("g", 4, 5), ("g", 9, 4),
    ("g", 5, 5), ("g", 7, 5), ("g", 8, 5), ("g", 9, 5),
]
TURN = 384
VMEM_LIMIT = 60 * 2**20


class Place:
    def __init__(self):
        self.me = me = lax.axis_index("tensor")
        self.c = c = lax.rem(me, 2)
        self.y = y = lax.rem(me // 2, 2)
        self.z = z = me // 4
        self.low = z // 2
        odd = lax.rem(z, 2)
        self.mid = (z == 1) | (z == 2)
        self.end = (z == 0) | (z == 3)
        self.core = me + 1 - 2 * c
        self.across = me + 2 - 4 * y
        self.near_z = z + 1 - 2 * odd
        self.far_z = 3 - z
        self.other_mid = 2 - self.low
        self.other_end = 3 - 3 * self.low
        self.near = self.near_z * 4 + y * 2 + c
        self.far = self.far_z * 4 + y * 2 + c


class Wire:
    def __init__(self):
        self.owed = []

    def make(self, src, dst, send_sem, recv_sem, target):
        return pltpu.make_async_remote_copy(
            src_ref=src, dst_ref=dst, send_sem=send_sem, recv_sem=recv_sem,
            device_id={"tensor": target}, device_id_type=MESH,
        )

    def send(self, src, dst, send_sem, recv_sem, target, when=None):
        copy = self.make(src, dst, send_sem, recv_sem, target)
        if when is None:
            copy.start()
        else:
            pl.when(when)(copy.start)

    def arrived(self, like, recv_sem, target):
        self.make(like, like, recv_sem, recv_sem, target).wait_recv()

    def owe(self, like, send_sem, target, when=None):
        self.owed.append((when, self.make(like, like, send_sem, send_sem, target)))

    def flush(self):
        for when, copy in self.owed:
            if when is None:
                copy.wait_send()
            else:
                pl.when(when)(copy.wait_send)
        self.owed = []


class Gather:
    ops = 7

    def __init__(self, at, wire, order, own, buf, sems):
        self.at, self.wire, self.order, self.own, self.buf = at, wire, order, own, buf
        self.zn, self.zf, self.ys, self.yr, self.cs, self.cr, self.ls = (sems.at[i] for i in range(7))
        self.zr = [sems.at[7 + i] for i in range(3)]

    def row(self, z):
        if self.order == "A":
            return self.buf.at[z, self.at.y, self.at.c]
        return self.buf.at[z, :, self.at.c]

    def z_copy(self, z, land, target, src=None):
        row = self.row(z)
        sem = self.zn if target is self.at.near else self.zf
        return self.wire.make(row if src is None else src, row, sem, self.zr[land], target)

    def z_wait(self, z, land):
        self.wire.arrived(self.row(z), self.zr[land], self.at.near)

    def y_copy(self, z, src=None):
        at = self.at
        row = self.buf.at[z, at.y, at.c]
        return self.wire.make(row if src is None else src, row, self.ys, self.yr, at.across)

    def c_send(self, part):
        self.wire.send(part, part, self.cs, self.cr, self.at.core)

    def keep(self):
        at = self.at
        return pltpu.make_async_copy(self.own, self.buf.at[at.z, at.y, at.c], self.ls)

    def debts(self):
        at, buf, owe = self.at, self.buf, self.wire.owe
        owe(buf.at[:, at.y, at.c] if self.order == "A" else buf.at[at.z, at.y, at.c], self.ys, at.across)
        owe(buf.at[:, :, at.c], self.cs, at.core)
        owe(self.row(at.z), self.zn, at.near, when=at.end)
        owe(self.row(pl.ds(0, 3)), self.zn, at.near, when=at.mid)
        owe(self.row(pl.ds(0, 2)), self.zf, at.far, when=at.mid)

    def op(self, k):
        at = self.at
        if self.order == "A":
            self.op_a(k, at)
        else:
            self.op_b(k, at)
        if k == 6:
            self.debts()

    def pass_on(self, who, z, land, target=None, there=None):
        copies = []
        if target is not None:
            copies.append(self.z_copy(z, there, target))
        if self.order == "A":
            copies.append(self.y_copy(z))

        @pl.when(who)
        def _():
            self.z_wait(z, land)
            for copy in copies:
                copy.start()

    def op_a(self, k, at):
        buf = self.buf
        if k == 0:
            self.z_copy(at.z, 0, at.near, src=self.own).start()
            pl.when(at.mid)(self.z_copy(at.z, 1, at.far, src=self.own).start)
            self.y_copy(at.z, src=self.own).start()
            self.keep().start()
        elif k == 1:
            self.z_wait(at.near_z, 0)
            pl.when(at.mid)(self.z_copy(at.near_z, 2, at.far).start)
            self.y_copy(at.near_z).start()
        elif k == 2:
            self.pass_on(at.mid, at.other_mid, 1, at.near, 1)
        elif k == 3:
            self.pass_on(at.mid, at.other_end, 2, at.near, 2)
            self.pass_on(at.end, at.other_mid, 1)
        elif k == 4:
            self.pass_on(at.end, at.other_end, 2)
            self.keep().wait()
            self.c_send(buf.at[:, at.y, at.c])
        elif k == 5:
            self.wire.arrived(buf.at[:, 1 - at.y, at.c], self.yr, at.across)
            self.c_send(buf.at[:, 1 - at.y, at.c])
        else:
            self.wire.arrived(buf.at[:, :, 1 - at.c], self.cr, at.core)

    def op_b(self, k, at):
        buf = self.buf
        if k == 0:
            self.y_copy(at.z, src=self.own).start()
            self.keep().start()
        elif k == 1:
            self.keep().wait()
            self.wire.arrived(buf.at[at.z, 1 - at.y, at.c], self.yr, at.across)
            self.z_copy(at.z, 0, at.near).start()
            pl.when(at.mid)(self.z_copy(at.z, 1, at.far).start)
        elif k == 2:
            self.pass_on(at.mid, at.near_z, 0, at.far, 2)
        elif k == 3:
            self.pass_on(at.mid, at.other_mid, 1, at.near, 1)
        elif k == 4:
            self.pass_on(at.mid, at.other_end, 2, at.near, 2)
        elif k == 5:

            @pl.when(at.end)
            def _():
                self.z_wait(at.near_z, 0)
                self.z_wait(at.other_mid, 1)
                self.z_wait(at.other_end, 2)

            self.c_send(buf.at[:, :, at.c])
        else:
            self.wire.arrived(buf.at[:, :, 1 - at.c], self.cr, at.core)


class Reduce:
    ops = 6

    def __init__(self, at, wire, order, part, fill, finish, bufs, sems):
        self.at, self.wire, self.order = at, wire, order
        self.part, self.fill, self.finish = part, fill, finish
        self.r1, self.s1, self.yb, self.r2, self.go, self.rn, self.rf = bufs
        self.cs, self.ys, self.yr, self.ns, self.nr, self.fs, self.fr = (sems.at[i] for i in range(7))
        self.cr = [sems.at[7 + i] for i in range(2)]

    def debts(self):
        at, owe = self.at, self.wire.owe
        owe(self.r1, self.cs, at.core)
        owe(self.s1 if self.order == "A" else self.yb, self.ys, at.across)
        owe(self.go, self.ns, at.near, when=at.end)
        owe(self.go.at[pl.ds(2, 1)], self.ns, at.near, when=at.mid)
        owe(self.go.at[pl.ds(0, 2)], self.fs, at.far, when=at.mid)

    def op(self, k):
        at = self.at
        if k == 0:
            self.begin(at)
        elif self.order == "A":
            self.op_a(k, at)
        else:
            self.op_b(k, at)
        if k == 5:
            self.debts()

    def begin(self, at):
        self.fill()
        for i, y in enumerate((1 - at.y, at.y)):
            self.wire.send(self.part(y, 1 - at.c), self.r1.at[y], self.cs, self.cr[i], at.core)

    def c_wait(self, at, i):
        y = (1 - at.y, at.y)[i]
        self.wire.arrived(self.r1.at[y], self.cr[i], at.core)

    def two(self, y, zs):
        at = self.at
        return self.part(y, at.c)[zs].astype(f32) + self.r1[y, zs].astype(f32)

    def total(self, zs):
        at = self.at
        if self.order == "A":
            return self.two(at.y, zs) + self.r2[zs].astype(f32)
        return jnp.stack([self.two(y, zs) for y in range(2)], axis=1)

    def z_ops(self, k, at):
        go, rn, rf = self.go, self.rn, self.rf
        if k == 0:
            inward = self.wire.make(go, rn, self.ns, self.nr, at.near)

            @pl.when(at.end)
            def _():
                go[...] = self.total(pl.ds(1 - at.low, 3)).astype(bf16)
                inward.start()

        elif k == 1:
            onward = self.wire.make(go.at[pl.ds(0, 2)], rf, self.fs, self.fr, at.far)

            @pl.when(at.mid)
            def _():
                self.wire.arrived(rn, self.nr, at.near)
                there = self.total(pl.ds(2 - 2 * at.low, 2))
                go[0:2] = (there + rn[pl.ds(1 - at.low, 2)].astype(f32)).astype(bf16)
                onward.start()

        elif k == 2:
            back = self.wire.make(go.at[pl.ds(2, 1)], rn.at[pl.ds(0, 1)], self.ns, self.nr, at.near)

            @pl.when(at.mid)
            def _():
                self.wire.arrived(rf, self.fr, at.far)
                there = self.total(pl.ds(at.near_z, 1))
                go[2:3] = (there + rf[pl.ds(at.low, 1)].astype(f32)).astype(bf16)
                back.start()

    def own(self, at, done):
        rn, rf = self.rn, self.rf

        @pl.when(at.end)
        def _():
            self.wire.arrived(rn.at[pl.ds(0, 1)], self.nr, at.near)
            done((self.total(pl.ds(at.z, 1)) + rn[0:1].astype(f32))[0])

        @pl.when(at.mid)
        def _():
            done(
                (
                    self.total(pl.ds(at.z, 1))
                    + rn[pl.ds(2 * at.low, 1)].astype(f32)
                    + rf[pl.ds(1 - at.low, 1)].astype(f32)
                )[0]
            )

    def op_a(self, k, at):
        every = pl.ds(0, 4)
        if k == 1:
            self.c_wait(at, 0)
            self.s1[...] = self.two(1 - at.y, every).astype(bf16)
            self.wire.send(self.s1, self.r2, self.ys, self.yr, at.across)
        elif k == 2:
            self.c_wait(at, 1)
            self.wire.arrived(self.r2, self.yr, at.across)
            self.z_ops(0, at)
        elif k == 3:
            self.z_ops(1, at)
        elif k == 4:
            self.z_ops(2, at)
        else:
            self.own(at, self.finish)

    def op_b(self, k, at):
        if k == 1:
            self.c_wait(at, 0)
            self.c_wait(at, 1)
            self.z_ops(0, at)
        elif k == 2:
            self.z_ops(1, at)
        elif k == 3:
            self.z_ops(2, at)
        elif k == 4:

            def store(v):
                self.s1[...] = v

            self.own(at, store)
            self.yb[...] = self.s1[1 - at.y].astype(bf16)
            self.wire.send(self.yb, self.r2, self.ys, self.yr, at.across)
        else:
            self.wire.arrived(self.r2, self.yr, at.across)
            self.finish(self.s1[at.y] + self.r2[...].astype(f32))


def reduce_scratch(order, r, n):
    V = pltpu.VMEM
    D = pltpu.SemaphoreType.DMA
    two = () if order == "A" else (2,)
    bufs = [
        V((2, 4, r, n), bf16),
        V((4, r, n), bf16) if order == "A" else V((2, r, n), f32),
        V((16, 128) if order == "A" else (r, n), bf16),
        V((4, r, n), bf16) if order == "A" else V((r, n), bf16),
        V((3,) + two + (r, n), bf16), V((3,) + two + (r, n), bf16), V((2,) + two + (r, n), bf16),
    ]
    return bufs, D((9,))


def gather_scratch(n):
    D = pltpu.SemaphoreType.DMA
    return [pltpu.VMEM((4, 2, 2, 32, n), bf16)], D((10,))


def cut(pieces, whole):
    starts, at = [], 0
    for size, order in pieces:
        starts.append((at, size, order))
        at += size
    return starts if at == whole else None


def plan(K, S, F):
    return cut(TEACHER, K), cut(STUDENT, S), cut(DOWN, F), cut(GRAD, S)


def body(dims, shapes, *refs):
    x, st, gate, up, down, gain, proj, ct, sa, sg, loss = refs[:11]
    take = iter(jax.tree.unflatten(shapes, refs[11:]))
    K, N, S, F, pad, fpad = dims
    teacher, student, downs, grads = plan(K, S, F)
    xa, xsems, xs, ssems, rbuf, rsem, qbuf, parts, wt = (next(take) for _ in range(9))
    (acc, hidden, wbuf, dbuf, ffn, base, gcol, projected, pbuf, gbuf, cot_t, cot,
     nb, nr, lb, lr, wsem, dsem, psem, gsem, osem, ns_, nr_, ls_, lr_) = take
    at, wire = Place(), Wire()
    B = x.shape[0]
    T = 16
    R = T * B
    turns = K // TURN
    me = at.me

    def fetch(j):
        first, n, _ = teacher[j]
        return [
            pltpu.make_async_copy(
                w.at[:, pl.ds(first, n)], wbuf.at[i, j % 2, :, pl.ds(0, n)], wsem.at[i, j % 2]
            )
            for i, w in enumerate((gate, up))
        ]

    def fetch_down(i):
        return pltpu.make_async_copy(
            down.at[:, pl.ds(i * TURN, TURN)], dbuf.at[i % 2, pl.ds(0, N)], dsem.at[i % 2]
        )

    projector = pltpu.make_async_copy(proj, pbuf.at[pl.ds(0, F)], psem)
    gains = pltpu.make_async_copy(gain, gbuf, gsem)

    for j in range(2):
        for copy in fetch(j):
            copy.start()
        fetch_down(j).start()
    projector.start()
    gains.start()
    others = [lax.rem(me + k, T) for k in range(1, T)]
    barrier = pltpu.get_barrier_semaphore()
    for target in others:
        pl.semaphore_signal(barrier, inc=1, device_id={"tensor": target}, device_id_type=MESH)
    pl.semaphore_wait(barrier, T - 1)

    gathers = [
        Gather(at, Wire(), order, x.at[:, pl.ds(first, n)], xa[j], xsems[j])
        for j, (first, n, order) in enumerate(teacher)
    ] + [
        Gather(at, wire, order, st.at[:, pl.ds(first, n)], xs[j], ssems[j])
        for j, (first, n, order) in enumerate(student)
    ]

    def clear():
        dbuf[:, N:pad] = jnp.zeros((2, pad - N, TURN), bf16)
        hidden[N:pad] = jnp.zeros((pad - N, R), bf16)
        pbuf[F:fpad] = jnp.zeros((fpad - F, S), bf16)
        cot_t[F:fpad] = jnp.zeros((fpad - F, R), bf16)
        base[...] = jnp.zeros_like(base)
        gcol[...] = jnp.zeros_like(gcol)

    def held(which, part):
        return acc.at[which * 4 + part]

    def multiply(j, i):
        first, n, _ = teacher[j]
        if i == 0:
            for copy in fetch(j):
                copy.wait()

        @pl.loop(0, 1)
        def _(_):
            d = lax.dot_general(
                wbuf[i, j % 2, :, 0:n], xa[j][...].reshape(R, n), by_last, preferred_element_type=f32
            )
            for q in range(4):
                part = d[q * F : (q + 1) * F]
                place = held(i, q)
                if j > 0:
                    part += place[...]
                if j < len(teacher) - 1 or i == 0:
                    place[...] = part
                else:
                    value = held(0, q)[...]
                    hidden[q * F : (q + 1) * F] = (
                        jax.nn.gelu(value, approximate=True) * part
                    ).astype(bf16)

        if i == 1:
            own_part(j)
            if j + 2 < len(teacher):
                for copy in fetch(j + 2):
                    copy.start()

    def one(rows, cols, off):
        i = lax.broadcasted_iota(jnp.int32, (rows, cols), 0)
        k = lax.broadcasted_iota(jnp.int32, (rows, cols), 1)
        return jnp.where(i == k + off, 1.0, 0.0).astype(bf16)

    def turn(i):
        fetch_down(i).wait()
        got = dbuf[i % 2].T
        row = 0
        while row < TURN:
            d, r = divmod(i * TURN + row, F)
            j = max(q for q, (first, _, _) in enumerate(downs) if first <= r)
            first, size, _ = downs[j]
            run = min(TURN - row, first + size - r)
            begin = d * size + r - first
            wt[j][begin : begin + run] = got[row : row + run]
            row += run
        if i + 2 < turns:
            fetch_down(i + 2).start()

    def own_part(j):
        first, n, _ = teacher[j]

        @pl.when((first < F * me + F) & (first + n > F * me))
        def _():
            sel = one(F, n, first - F * me)
            base[...] += lax.dot_general(
                sel, xa[j][...].reshape(R, n), by_last, preferred_element_type=f32
            )
            wide = jnp.broadcast_to(gbuf[first : first + n][None], (128, n))
            gcol[...] += lax.dot_general(sel, wide, by_last, preferred_element_type=f32)

    def project(j):
        first, n, _ = student[j]
        got = lax.dot_general(
            pbuf[0:F, first : first + n], xs[j][...].reshape(R, n), by_last,
            preferred_element_type=f32,
        )
        projected[...] = got if j == 0 else projected[...] + got
        outs.append(pltpu.make_async_copy(xs[j], sa.at[j], osem.at[1 + j]))
        outs[-1].start()

    def down_item(j):
        first, r, order = downs[j]

        held_by = parts[j] if j in parts else xa[j]

        def fill():
            if j not in parts:
                gathers[j].wire.flush()

            @pl.loop(0, 1)
            def _(_):
                got = jnp.dot(wt[j][...], hidden[...], preferred_element_type=f32)
                held_by[...] = got.astype(bf16).reshape(4, 2, 2, r, R)

        def finish(v):
            ffn[first : first + r] = v

        return Reduce(at, wire, order, lambda y, c: held_by.at[:, y, c], fill, finish, rbuf[j], rsem[j])

    def grad_item(j):
        first, n, order = grads[j]

        def fill():
            @pl.loop(0, 1)
            def _(_):
                got = jnp.dot(cot[...], pbuf[:, first : first + n], preferred_element_type=f32)
                xa[j][:, :, :, :, 0:n] = got.astype(bf16).reshape(4, 2, 2, B, n)

        def finish(v):
            sg[:, first : first + n] = v.astype(bf16)

        return Reduce(
            at, wire, order, lambda y, c: xa[j].at[:, y, c, :, pl.ds(0, n)], fill, finish,
            qbuf[j], rsem[j],
        )

    down_items = [down_item(j) for j in range(len(downs))]
    grad_items = [grad_item(j) for j in range(len(grads))]

    def everyone(src, dst, ss, rs):
        for v in others:
            wire.send(src, dst.at[me], ss, rs, v)
        dst[me] = src[...]
        wire.owe(dst.at[pl.ds(0, T - 1)], ss, others[0])

        def collect():
            wire.arrived(dst.at[pl.ds(0, T - 1)], rs, others[0])
            return jnp.sum(dst[...], axis=0)

        return collect

    def norm():
        whole = ffn[...]
        nb[...] = jnp.sum(whole * whole, axis=0, keepdims=True)
        collect = everyone(nb, nr, ns_, nr_)
        for gather in gathers:
            gather.wire.flush()
        wire.flush()
        inv_norm = lax.rsqrt(collect() / K + epsilon)
        target = (base[...] + ffn[...] * inv_norm * gcol[:, 0:1]).astype(bf16)
        difference = projected[...] - target.astype(f32)
        cot_t[0:F] = difference.astype(bf16)
        cot[...] = cot_t[...].T
        outs.append(pltpu.make_async_copy(cot_t.at[pl.ds(0, F)], ct, osem.at[0]))
        outs[-1].start()
        lb[...] = jnp.sum(difference * difference, axis=0, keepdims=True)

    calls = {
        "t": lambda j, k: gathers[j].op(k),
        "s": lambda j, k: gathers[len(teacher) + j].op(k),
        "d": lambda j, k: down_items[j].op(k),
        "g": lambda j, k: grad_items[j].op(k),
        "mul": multiply,
        "turn": lambda j, k: turn(j),
        "project": lambda j, k: project(j),
    }
    started = False
    outs = []
    for what, j, k in ORDER:
        if what not in ("t", "s") and not started:
            started = True
            clear()
            projector.wait()
            gains.wait()
        if what == "norm":
            norm()
        elif what == "loss":
            errors = everyone(lb, lr, ls_, lr_)
        else:
            calls[what](j, k)
    loss[...] = jnp.broadcast_to(jnp.sum(errors(), axis=1, keepdims=True) / (R * K), loss.shape)
    wire.flush()
    for copy in outs:
        copy.wait()


def distill(x, st, gate, up, down, gain, proj):
    B, K = x.shape
    N = gate.shape[0]
    S, F = st.shape[1], proj.shape[0]
    T = 16
    R = T * B
    pad, fpad = -(-N // 128) * 128, -(-F // 128) * 128
    teacher, student, downs, grads = plan(K, S, F)
    V = pltpu.VMEM
    D = pltpu.SemaphoreType.DMA
    widest = max(n for _, n, _ in teacher)
    xa = [gather_scratch(n) for _, n, _ in teacher]
    xs = [gather_scratch(n) for _, n, _ in student]
    rs = [reduce_scratch(order, r, R) for _, r, order in downs]
    qs = [reduce_scratch(order, B, n) for _, n, order in grads]
    scratch = [
        [b[0] for b, _ in xa], [s for _, s in xa],
        [b[0] for b, _ in xs], [s for _, s in xs],
        [b for b, _ in rs], [s for _, s in rs],
        [b for b, _ in qs],
        {j: V((4, 2, 2, r, R), bf16) for j, (_, r, _) in enumerate(downs) if not (j < len(teacher) and (B, R) == (r, teacher[j][1]))},
        [V((16 * r, pad), bf16) for _, r, _ in downs],
        V((8, F, R), f32), V((pad, R), bf16), V((2, 2, N, widest), bf16), V((2, pad, TURN), bf16),
        V((F, R), f32), V((F, R), f32), V((F, 128), f32), V((F, R), f32),
        V((fpad, S), bf16), V((K,), bf16), V((fpad, R), bf16), V((R, fpad), bf16),
        V((1, R), f32), V((T, 1, R), f32), V((1, R), f32), V((T, 1, R), f32),
        D((2, 2)), D((2,)), D(()), D(()), D((1 + len(student),)), D(()), D(()), D(()), D(()),
    ]
    flat, _ = jax.tree.flatten(scratch, is_leaf=lambda s: not isinstance(s, (list, dict)))
    shapes = jax.tree.structure(scratch, is_leaf=lambda s: not isinstance(s, (list, dict)))
    hbm = pl.BlockSpec(memory_space=pl.ANY)
    return pl.pallas_call(
        functools.partial(body, (K, N, S, F, pad, fpad), shapes),
        out_shape=[
            jax.ShapeDtypeStruct((F, R), bf16),
            jax.ShapeDtypeStruct((len(student), 4, 2, 2, B, student[0][1]), bf16),
            jax.ShapeDtypeStruct((B, S), bf16),
            jax.ShapeDtypeStruct((8, 128), f32),
        ],
        in_specs=[hbm] * 7,
        out_specs=[
            hbm,
            hbm,
            pl.BlockSpec(memory_space=pltpu.VMEM),
            pl.BlockSpec(memory_space=pltpu.VMEM),
        ],
        scratch_shapes=flat,
        name="distill",
        cost_estimate=pl.CostEstimate(
            flops=6 * R * K * N + 6 * R * S * F,
            bytes_accessed=6 * K * N + 6 * S * F,
            transcendentals=0,
        ),
        compiler_params=pltpu.CompilerParams(
            collective_id=1, has_side_effects=True, vmem_limit_bytes=VMEM_LIMIT
        ),
    )(x, st, gate, up, down, gain, proj)


def finish_kernel(ct, sa, sg, loss, out_loss, out_pg, out_sg, xbuf, pbuf, isem, osem, gsem):
    J, R, n = xbuf.shape[0], ct.shape[1], xbuf.shape[-1]
    student = pltpu.make_async_copy(sg, out_sg, gsem)
    arrive = [pltpu.make_async_copy(sa.at[j], xbuf.at[j], isem.at[j]) for j in range(J)]
    leave = [
        pltpu.make_async_copy(pbuf.at[j], out_pg.at[:, pl.ds(j * n, n)], osem.at[j]) for j in range(J)
    ]
    for copy in arrive:
        copy.start()
    student.start()
    out_loss[0] = loss[0, 0]
    for j in range(J):
        arrive[j].wait()
        pbuf[j] = jnp.dot(ct[...], xbuf[j].reshape(R, n), preferred_element_type=f32)
        leave[j].start()
    student.wait()
    for copy in leave:
        copy.wait()


def finish(ct, sa, sg, loss):
    F, R = ct.shape
    J, n = sa.shape[0], sa.shape[-1]
    vm, hbm = (pl.BlockSpec(memory_space=space) for space in (pltpu.VMEM, pl.ANY))
    D = pltpu.SemaphoreType.DMA
    return pl.pallas_call(
        finish_kernel,
        out_shape=[
            jax.ShapeDtypeStruct((1,), f32),
            jax.ShapeDtypeStruct((F, J * n), f32),
            jax.ShapeDtypeStruct(sg.shape, bf16),
        ],
        in_specs=[vm, hbm, hbm, vm],
        out_specs=[pl.BlockSpec(memory_space=pltpu.SMEM), hbm, hbm],
        scratch_shapes=[
            pltpu.VMEM(sa.shape, bf16), pltpu.VMEM((J, F, n), f32), D((J,)), D((J,)), D(()),
        ],
        name="finish",
        cost_estimate=pl.CostEstimate(
            flops=2 * R * F * J * n, bytes_accessed=2 * R * J * n + 4 * F * J * n, transcendentals=0
        ),
        compiler_params=pltpu.CompilerParams(vmem_limit_bytes=VMEM_LIMIT),
    )(ct, sa, sg, loss)


def local(teacher_in, gate_weight, up_weight, down_weight, post_gain, student_in, proj_weight):
    width_count = lax.axis_size("tensor")
    K, S, F = teacher_in.shape[1], student_in.shape[1], proj_weight.shape[0]
    fits = (
        width_count == 16
        and teacher_in.shape[0] == 32
        and gate_weight.shape[0] == 4 * F
        and S == 5 * 32 * width_count
        and K == width_count * F
        and K % TURN == 0
        and None not in plan(K, S, F)
    )
    if fits:
        return finish(*distill(
            teacher_in, student_in, gate_weight, up_weight, down_weight, post_gain, proj_weight
        ))
    contract_last = (((1,), (1,)), ((), ()))
    block_rows = lax.all_gather(teacher_in, "tensor", axis=0, tiled=True)
    gate_value = lax.dot_general(
        block_rows, gate_weight, contract_last, preferred_element_type=jnp.float32
    )
    lift_value = lax.dot_general(
        block_rows, up_weight, contract_last, preferred_element_type=jnp.float32
    )
    hidden = (jax.nn.gelu(gate_value, approximate=True) * lift_value).astype(jnp.bfloat16)
    student_all = lax.all_gather(student_in, "tensor", axis=0, tiled=True)
    ffn_out = lax.psum_scatter(
        jnp.dot(hidden, down_weight, preferred_element_type=jnp.float32),
        "tensor",
        scatter_dimension=0,
        tiled=True,
    )
    inv_norm = lax.rsqrt(jnp.mean(ffn_out * ffn_out, axis=-1, keepdims=True) + epsilon)
    target_rows = (
        teacher_in.astype(jnp.float32) + ffn_out * inv_norm * post_gain.astype(jnp.float32)
    ).astype(jnp.bfloat16)
    target = lax.all_to_all(target_rows, "tensor", split_axis=1, concat_axis=0, tiled=True)
    projected = lax.dot_general(
        student_all, proj_weight, contract_last, preferred_element_type=jnp.float32
    )
    difference = projected - target.astype(jnp.float32)
    squares = jnp.sum(difference * difference)
    cotangent = difference.astype(jnp.bfloat16)
    proj_grad = lax.dot_general(
        cotangent, student_all, (((0,), (0,)), ((), ())), preferred_element_type=jnp.float32
    )
    total_error = lax.psum(squares, "tensor")
    student_grad = lax.psum_scatter(
        jnp.dot(cotangent, proj_weight, preferred_element_type=jnp.float32),
        "tensor",
        scatter_dimension=0,
        tiled=True,
    ).astype(jnp.bfloat16)
    loss_value = total_error / (student_all.shape[0] * proj_weight.shape[0] * width_count)
    return (jnp.reshape(loss_value, (1,)), proj_grad, student_grad)


def solution(mesh):
    placed = (
        P(("groups", "tensor"), None),
        P("tensor", None),
        P("tensor", None),
        P("tensor", None),
        P(),
        P(("groups", "tensor"), None),
        P("tensor", None),
    )
    return jax.shard_map(
        local,
        mesh=mesh,
        in_specs=placed,
        out_specs=(P("groups"), P(("groups", "tensor"), None), P(("groups", "tensor"), None)),
        check_vma=False,
    )
```
